256 devices in a mesh: inline: 32 (over z, y_lo, core), shot: 8 (over y_hi, x).
Axes of the slice: x: 4, y: 4 (y_hi: 2, y_lo: 2; y = y_hi * 2 + y_lo), z: 8, core: 2. Of those that a mesh axis runs over, the one named last changes fastest.
Arguments:
- source: bfloat16 [32, 1024, 32, 256], P('shot', 'inline'), may hold values from -6 to 6
- receiver: bfloat16 [32, 1024, 32, 256], P('shot', 'inline'), may hold values from -6 to 6
Outputs:
- offset_image: float32 [129, 1024, 256], P(None, 'inline', 'shot')
The draws below stay inside these ranges and needn't reach their ends.
All inputs are finite; a program needn't handle non-finite values.
Results may differ from the reference program's by a relative error of at most 0.0003.
Values may be sent and summed in bfloat16 or wider, within the bound.
A program may use at most 192 MiB of HBM per device.

```python
import jax
import jax.numpy as jnp
from jax import lax

HLAG = 64
NY = 256
NT = 32
CX = 32
NX = 1024
SHOTS = 32


def spiked(array, key, source, target, parts, factor):
    owner, partner = [(jnp.arange(array.shape[position]) // (array.shape[position] // parts)).reshape([-1 if axis == position else 1 for axis in range(array.ndim)]) for position in (source, target)]
    chosen = jax.random.permutation(key, parts)[partner]
    strong = (owner == chosen) | (owner == (partner + parts // 2) % parts)
    return jnp.where(strong, factor * array, array)


def levels(own_key, shape, pieces, least, top_value):
    def one(dim, blocks):
        heights = jax.random.uniform(jax.random.fold_in(jax.random.fold_in(own_key, 6), dim), (blocks,), jnp.float32, least / len(pieces), top_value / len(pieces))
        return jnp.repeat(jnp.exp(heights), shape[dim] // blocks).reshape((-1,) + (1,) * (len(shape) - dim - 1))

    loudness = one(*pieces[0])
    for cut in pieces[1:]:
        loudness = loudness * one(*cut)
    return loudness


def centred(stream_key, dims, deviation, bound, shards=(), held_as=jnp.bfloat16):
    loudness = levels(stream_key, dims, shards, -0.22, 0.18) if shards else 1.0
    values = jax.random.normal(stream_key, dims, jnp.float32) * deviation * loudness
    return jnp.minimum(jnp.maximum(values, -bound), bound).astype(held_as)


def bell_draw_with(own_key, dims, spread, limit, cuts, heavy, kind=jnp.bfloat16):
    entries = spread * jax.random.normal(own_key, dims, jnp.float32)
    if cuts:
        entries = entries * levels(own_key, dims, cuts, -0.22, 0.18)
    return jnp.clip(spiked(entries, jax.random.fold_in(own_key, 3), *heavy), -limit, limit).astype(kind)


def setup_inputs(seed: int = 0) -> dict:
    streams_of = jax.random.split(jax.random.key(seed), 3)
    return {
        "source": centred(streams_of[0], (SHOTS, NX, NT, NY), 1.0, 6.0, ((0, 8), (1, 32))),
        "receiver": bell_draw_with(streams_of[1], (SHOTS, NX, NT, NY), 1.0, 6.0, ((0, 8), (1, 32)), (0, 3, 8, 2.0)),
    }


def band_of(product, width, lags):
    rows = product.shape[1]
    flat = product.reshape(product.shape[0], rows * width)
    flat = jnp.pad(flat, ((0, 0), (0, rows)))
    skewed = flat.reshape(product.shape[0], rows, width + 1)[:, :, :lags]
    return jnp.transpose(skewed, (2, 1, 0))


def reference(source, receiver):
    padded = jnp.pad(receiver, ((0, 0), (HLAG, HLAG), (0, 0), (0, 0)))
    width = CX + 2 * HLAG

    def one_block(block):
        start = (block * CX).astype(jnp.int32)
        left = lax.dynamic_slice_in_dim(source, start, CX, 1).astype(jnp.float32)
        right = lax.dynamic_slice_in_dim(padded, start, width, 1).astype(jnp.float32)
        product = jnp.einsum("sity,szty->yiz", left, right, precision=lax.Precision.HIGHEST)
        return band_of(product, width, 2 * HLAG + 1)

    blocks = lax.map(one_block, jnp.arange(NX // CX, dtype=jnp.int32))
    image = jnp.transpose(blocks, (1, 0, 2, 3)).reshape(2 * HLAG + 1, NX, NY)
    return image * (1.0 / (NT * SHOTS) ** 0.5)
```

```python
import functools

import jax
import jax.numpy as jnp
from jax import lax
from jax.experimental import pallas as pl
from jax.experimental.pallas import tpu as pltpu
from jax.sharding import PartitionSpec as P

MESH = pl.DeviceIdType.MESH
F32 = jnp.float32
BF16 = jnp.bfloat16
LANES = 128
RINGS = 4
HOPS = (2, 1, 3, 0)
STEPS = [(part, hop) for part in range(2) for hop in HOPS]
FAR_UP, FAR_DOWN, SUM_UP, SUM_DOWN, NEAR_UP, NEAR_DOWN = range(6)


def kernel(
    source, receiver, out,
    raw, turned, left, right, partial, inbox, across,
    raw_sem, halo_send, halo_recv, ring_send, ring_recv, across_send, across_recv,
):
    shots, cells, times, _ = source.shape
    block = left.shape[0] // 8
    half = block // 2
    owners = lax.axis_size("inline")
    me, shot = lax.axis_index("inline"), lax.axis_index("shot")
    core, low, x, high = me % 2, (me // 2) % 2, shot % RINGS, shot // RINGS
    core_mate = me + 1 - 2 * core
    low_mate = me + 2 - 4 * low
    along = (me + 4 - 8 * low + owners) % owners
    against = (me - 4 + 8 * low + owners) % owners
    up = high * RINGS + (x + 1) % RINGS
    down = high * RINGS + (x + RINGS - 1) % RINGS
    high_mate = (1 - high) * RINGS + x
    peers = [(core_mate, shot), (low_mate, shot), (along, shot), (against, shot), (me, up), (me, down), (me, high_mate)]

    def place(inline, line):
        return {"inline": inline, "shot": line}

    def tile(part):
        return pl.multiple_of(((high + 1 + part) % 2) * LANES, LANES)

    def first(step):
        part, hop = STEPS[step]
        return tile(part) + ((x + hop) % RINGS) * block

    loads = []
    for part in range(2):
        for which, array in enumerate((receiver, source)):
            loads.append(
                pltpu.make_async_copy(
                    array.at[:, :, :, pl.ds(tile(part), LANES)], raw.at[part, which], raw_sem.at[part, which]
                )
            )
            loads[-1].start()

    barrier = pltpu.get_barrier_semaphore()
    for inline, line in peers:
        pl.semaphore_signal(barrier, inc=1, device_id=place(inline, line), device_id_type=MESH)

    def relayout(part, which):
        loads[2 * part + which].wait()

        def turn(i, carry):
            rows = jnp.concatenate([raw[part, which, s, i].astype(F32) for s in range(shots)], axis=0)
            row = cells - 1 - i if which else i
            turned[pl.ds(pl.multiple_of(row * LANES, LANES), LANES), :] = rows.T
            return carry

        def gather(y, carry):
            value = turned[pl.ds(y, cells, stride=LANES), :].astype(BF16)
            if which:
                left[tile(part) + y] = value
            else:
                right[2, tile(part) + y] = value
            return carry

        lax.fori_loop(0, cells, turn, 0, unroll=2)
        lax.fori_loop(0, LANES, gather, 0, unroll=8)

    def halo(kind, step, slot, target_slot, inline):
        rows = pl.ds(first(step), block)
        return pltpu.make_async_remote_copy(
            src_ref=right.at[slot, rows],
            dst_ref=right.at[target_slot, rows],
            send_sem=halo_send.at[kind, step],
            recv_sem=halo_recv.at[kind, step],
            device_id=place(inline, shot),
            device_id_type=MESH,
        )

    def own_core(step):
        return halo(0, step, 2, 1 + 2 * core, core_mate)

    def own_low(step):
        return halo(1, step, 2, 4 * low, low_mate)

    def relay_along(step):
        return halo(2, step, 4 * (1 - low), 4 * low, along)

    def relay_core(step):
        return halo(3, step, 4 * (1 - core), 3 - 2 * core, core_mate)

    def ring(kind, part, step, which, line):
        return pltpu.make_async_remote_copy(
            src_ref=partial.at[step, which],
            dst_ref=inbox.at[part, kind],
            send_sem=ring_send.at[part, kind],
            recv_sem=ring_recv.at[part, kind],
            device_id=place(me, line),
            device_id_type=MESH,
        )

    lane = lax.broadcasted_iota(jnp.int32, (cells, LANES), 1)
    row = lax.broadcasted_iota(jnp.int32, (cells, LANES), 0)
    inside = (lane >= cells * (2 - me)) & (lane < cells * (owners + 2 - me))
    beyond = lane < cells * (owners + 2 - me) - LANES
    straight = lane < LANES - cells + 1 + row

    def correlate(step, which, added=None):
        start = first(step) + which * half

        def one(m, edge):
            y = start + m
            s = left[y]
            near = jnp.concatenate([right[slot, y] for slot in range(4)], axis=0)
            contract = (((1,), (1,)), ((), ()))
            a = lax.dot_general(s, near, contract, preferred_element_type=F32)
            b = lax.dot_general(s, right[4, y], contract, preferred_element_type=F32)
            b = jnp.concatenate([b, jnp.zeros((cells, LANES - cells), F32)], axis=1)
            a = jnp.where(inside, a, 0.0)
            b = jnp.where(beyond, b, 0.0)
            a = pltpu.roll(a, LANES - cells + 1, axis=1, stride=1, stride_axis=0)
            b = pltpu.roll(b, LANES - cells + 1, axis=1, stride=1, stride_axis=0)
            band = jnp.where(straight, a, b)
            if added is not None:
                band = band + added[m]
            partial[step, which, m] = band
            return jnp.where(lane == m, pltpu.roll(b, m, axis=1), edge)

        edge = lax.fori_loop(0, half, one, jnp.zeros((cells, LANES), F32), unroll=4)
        if added is not None:
            edge = edge + added[half]
        partial[step, which, half] = edge

    sent = []

    def go(copy):
        copy.start()
        sent.append(copy)
        return copy

    def process(step):
        own_core(step).wait_recv()
        relay_core(step).wait_recv()
        part, hop = STEPS[step]
        if hop == 2:
            correlate(step, 0)
            go(ring(FAR_UP, part, step, 0, up))
            correlate(step, 1)
            go(ring(FAR_DOWN, part, step, 1, down))
        elif hop == 1:
            correlate(step, 1)
            go(ring(NEAR_UP, part, step, 1, up))
            ring(FAR_UP, part, step, 0, up).wait_recv()
            correlate(step, 0, inbox.at[part, FAR_UP])
            go(ring(SUM_UP, part, step, 0, up))
        elif hop == 3:
            correlate(step, 0)
            go(ring(NEAR_DOWN, part, step, 0, down))
            ring(FAR_DOWN, part, step, 1, down).wait_recv()
            correlate(step, 1, inbox.at[part, FAR_DOWN])
            go(ring(SUM_DOWN, part, step, 1, down))
        else:
            correlate(step, 0)
            correlate(step, 1)

    def gather_ring(part):
        step = STEPS.index((part, 0))
        for kind, which in ((SUM_UP, 0), (NEAR_DOWN, 0), (SUM_DOWN, 1), (NEAR_UP, 1)):
            ring(kind, part, step, which, up).wait_recv()

        def add(m, carry):
            for which, kinds in enumerate(((SUM_UP, NEAR_DOWN), (SUM_DOWN, NEAR_UP))):
                total = partial[step, which, m] + inbox[part, kinds[0], m] + inbox[part, kinds[1], m]
                if part:
                    total = total + across[which, m]
                partial[step, which, m] = total
            return carry

        if part:
            exchange().wait_recv()
        lax.fori_loop(0, half + 1, add, 0)

    def exchange():
        return pltpu.make_async_remote_copy(
            src_ref=partial.at[STEPS.index((0, 0))],
            dst_ref=across,
            send_sem=across_send,
            recv_sem=across_recv,
            device_id=place(me, high_mate),
            device_id_type=MESH,
        )

    relayout(0, 0)
    pl.semaphore_wait(barrier, len(peers))
    for step in range(4):
        go(own_low(step))
        go(own_core(step))
    relayout(0, 1)
    relayout(1, 0)
    for step in range(4, 8):
        go(own_low(step))
        go(own_core(step))

    def forward(step):
        own_low(step).wait_recv()
        go(relay_along(step))

    def share(step):
        relay_along(step).wait_recv()
        go(relay_core(step))

    forward(0)
    relayout(1, 1)
    forward(1)
    share(0)
    for step in range(8):
        if step + 2 < 8:
            forward(step + 2)
        if step + 1 < 8:
            share(step + 1)
        process(step)
        if step == 4:
            gather_ring(0)
            go(exchange())
    gather_ring(1)

    last = STEPS.index((1, 0))
    total = partial.at[last]
    for which in range(2):
        edge = total[which, half].T
        rows = pl.ds(which * half, half)
        for i in range(cells):
            back = cells - 1 - i
            out[i, rows, 0:LANES] = total[which, 0:half, back, :]
            out[i, rows, LANES : LANES + 1] = edge[0:half, back : back + 1]
    for copy in sent:
        copy.wait_send()


def on_device(source, receiver):
    shots, cells, times, cross = source.shape
    all_shots = shots * lax.axis_size("shot")
    block = cross // 8
    half = block // 2
    scale = 1.0 / (times * all_shots) ** 0.5
    lags = 4 * cells + 1
    image = pl.pallas_call(
        kernel,
        out_shape=jax.ShapeDtypeStruct((cells, block, lags), F32),
        in_specs=[pl.BlockSpec(memory_space=pl.ANY)] * 2,
        out_specs=pl.BlockSpec(memory_space=pltpu.VMEM),
        scratch_shapes=[
            pltpu.VMEM((2, 2, shots, cells, times, LANES), BF16),
            pltpu.VMEM((cells * LANES, LANES), F32),
            pltpu.VMEM((cross, cells, LANES), BF16),
            pltpu.VMEM((5, cross, cells, LANES), BF16),
            pltpu.VMEM((8, 2, half + 1, cells, LANES), F32),
            pltpu.VMEM((2, 6, half + 1, cells, LANES), F32),
            pltpu.VMEM((2, half + 1, cells, LANES), F32),
            pltpu.SemaphoreType.DMA((2, 2)),
            pltpu.SemaphoreType.DMA((4, 8)),
            pltpu.SemaphoreType.DMA((4, 8)),
            pltpu.SemaphoreType.DMA((2, 6)),
            pltpu.SemaphoreType.DMA((2, 6)),
            pltpu.SemaphoreType.DMA,
            pltpu.SemaphoreType.DMA,
        ],
        compiler_params=pltpu.CompilerParams(collective_id=0, has_side_effects=True, vmem_limit_bytes=60 * 2**20),
    )(source, receiver)
    return jnp.transpose(image * scale, (2, 0, 1))


def solution(mesh):
    placed = (P("shot", "inline", None, None), P("shot", "inline", None, None))
    return jax.shard_map(
        on_device, mesh=mesh, in_specs=placed, out_specs=P(None, "inline", "shot"), check_vma=False
    )
```

```python
import jax
import jax.numpy as jnp
from jax import lax
from jax.experimental import pallas as pl
from jax.experimental.pallas import tpu as pltpu
from jax.sharding import PartitionSpec as P

MESH = pl.DeviceIdType.MESH
F32 = jnp.float32
BF16 = jnp.bfloat16
LANES = 128
SUBLANES = 8
RINGS = 4
QUAD = 4
SIZES = (4, 4, 4, 2, 2)
STARTS = (0, 4, 8, 12, 14)
RISING = (True, False, True, False, False)
UNITS = (
    (0, 2), (1, 2), (2, 2), (3, 2), (4, 2), (0, 1), (1, 3), (1, 1), (0, 3), (2, 1),
    (3, 3), (3, 1), (4, 3), (2, 3), (4, 1), (0, 0), (1, 0), (2, 0), (3, 0), (4, 0),
)
FIRST = [sum(SIZES[piece] for piece, _ in UNITS[:unit]) for unit in range(len(UNITS))]
FAR, SUM, NEAR = range(3)
AHEAD = 2


def kernel(
    source, receiver, out,
    raw, turned, own, left, right, partial, inbox, across, total, total_edge, landed, landed_edge,
    raw_sem, own_sem, ship_send, ship_recv, along_send, along_recv, ring_send, ring_recv,
    over_send, over_recv, home_send, home_recv,
):
    shots, cells, times, _ = source.shape
    share = sum(SIZES)
    wide = QUAD * cells
    owners = lax.axis_size("inline")
    me, shot = lax.axis_index("inline"), lax.axis_index("shot")
    core, low, x, high = me % 2, (me // 2) % 2, shot % RINGS, shot // RINGS
    place_in_quad, z = me % QUAD, me // QUAD
    quad = z * QUAD
    core_mate = me + 1 - 2 * core
    low_mate = me + 2 - 4 * low
    above = (me + QUAD) % owners
    below = (me + owners - QUAD) % owners
    up = high * RINGS + (x + 1) % RINGS
    down = high * RINGS + (x + RINGS - 1) % RINGS
    high_mate = (1 - high) * RINGS + x
    diagonal = low_mate + 1 - 2 * core
    peers = [
        (core_mate, shot), (low_mate, shot), (diagonal, shot), (above, shot), (below, shot),
        (me, up), (me, down), (low_mate, high_mate),
    ]
    sums_here = low == core

    def place(inline, line):
        return {"inline": inline, "shot": line}

    loads = []
    for which, array in enumerate((receiver, source)):
        for tile in range(2):
            loads.append(
                pltpu.make_async_copy(
                    array.at[:, :, :, pl.ds(tile * LANES, LANES)], raw.at[which, tile], raw_sem.at[which, tile]
                )
            )
            loads[-1].start()

    barrier = pltpu.get_barrier_semaphore()
    for inline, line in peers:
        pl.semaphore_signal(barrier, inc=1, device_id=place(inline, line), device_id_type=MESH)

    def relayout(which, tile):
        loads[2 * which + tile].wait()

        def turn(i, carry):
            rows = jnp.concatenate([raw[which, tile, s, i].astype(F32) for s in range(shots)], axis=0)
            row = cells - 1 - i if which else i
            turned[pl.ds(pl.multiple_of(row * LANES, LANES), LANES), :] = rows.T
            return carry

        def gather(y, carry):
            own[which, tile * LANES + y] = turned[pl.ds(y, cells, stride=LANES), :].astype(BF16)
            return carry

        lax.fori_loop(0, cells, turn, 0, unroll=4)
        lax.fori_loop(0, LANES, gather, 0, unroll=16)

    def rows_from(unit, half, target_core):
        piece, hop = UNITS[unit]
        start = half * LANES + ((x + hop) % RINGS) * 2 * share + target_core * share + STARTS[piece]
        return pl.ds(start, SIZES[piece])

    def rows_to(unit):
        return pl.ds(FIRST[unit], SIZES[UNITS[unit][0]])

    def slot(which, unit):
        if which:
            return left.at[QUAD - 1 - place_in_quad, rows_to(unit)]
        return right.at[2 + place_in_quad, rows_to(unit)]

    def ship(which, unit, half, target, target_core, sent_as, received_as):
        return pltpu.make_async_remote_copy(
            src_ref=own.at[which, rows_from(unit, half, target_core)],
            dst_ref=slot(which, unit),
            send_sem=ship_send.at[which, sent_as, unit],
            recv_sem=ship_recv.at[which, received_as, unit],
            device_id=place(target, shot),
            device_id_type=MESH,
        )

    def to_mate(which, unit):
        return ship(which, unit, (low + high + 1 - core) % 2, core_mate, 1 - core, 0, 0)

    def to_other(which, unit, tile):
        target_core = (tile + 1 - low + high) % 2
        return ship(which, unit, tile, quad + 2 * (1 - low) + target_core, target_core, 1 + tile, 1 + core)

    def from_other(which, unit, sender):
        return ship(which, unit, 0, low_mate, core, 1, 1 + sender)

    def keep(which, unit):
        return pltpu.make_async_copy(
            own.at[which, rows_from(unit, (low + high + core) % 2, core)], slot(which, unit), own_sem.at[which, unit]
        )

    def extend(unit, upward):
        rows = rows_to(unit)
        begin, end = (4, 0) if upward else (2, 6)
        return pltpu.make_async_remote_copy(
            src_ref=right.at[pl.ds(begin, 2), rows],
            dst_ref=right.at[pl.ds(end, 2), rows],
            send_sem=along_send.at[int(upward), unit],
            recv_sem=along_recv.at[int(upward), unit],
            device_id=place(above if upward else below, shot),
            device_id_type=MESH,
        )

    def unit_rows(unit):
        return pl.ds(FIRST[unit] * wide + unit * SUBLANES, SIZES[UNITS[unit][0]] * wide + SUBLANES)

    def piece_rows(piece):
        return pl.ds(STARTS[piece] * wide + piece * SUBLANES, SIZES[piece] * wide + SUBLANES)

    def ring(kind, unit, line):
        piece, _ = UNITS[unit]
        return pltpu.make_async_remote_copy(
            src_ref=partial.at[unit_rows(unit)],
            dst_ref=inbox.at[kind, piece_rows(piece)],
            send_sem=ring_send.at[kind, piece],
            recv_sem=ring_recv.at[kind, piece],
            device_id=place(me, line),
            device_id_type=MESH,
        )

    lane = lax.broadcasted_iota(jnp.int32, (wide, LANES), 1)
    straight = lane <= lax.broadcasted_iota(jnp.int32, (wide, LANES), 0)

    def correlate(unit, kinds):
        piece, _ = UNITS[unit]
        size = SIZES[piece]
        begin, begin_in = FIRST[unit] * wide + unit * SUBLANES, STARTS[piece] * wide + piece * SUBLANES

        @pl.when(z == 0)
        def _():
            right[0:2, rows_to(unit)] = jnp.zeros((2, size, cells, LANES), BF16)

        @pl.when(z == owners // QUAD - 1)
        def _():
            right[6:8, rows_to(unit)] = jnp.zeros((2, size, cells, LANES), BF16)

        edge = jnp.zeros((wide, LANES), F32)
        for m in range(size):
            y = FIRST[unit] + m
            contract = (((1,), (1,)), ((), ()))
            rows = jnp.concatenate([left[part, y] for part in range(QUAD)], axis=0)
            columns = jnp.concatenate([right[part, y] for part in range(2 * QUAD)], axis=0)
            product = lax.dot_general(rows, columns, contract, preferred_element_type=F32)
            a = pltpu.roll(product[:, 0:LANES], 1, axis=1, stride=1, stride_axis=0)
            b = pltpu.roll(product[:, LANES:], 1, axis=1, stride=1, stride_axis=0)
            band = jnp.where(straight, a, b)
            for kind in kinds:
                band = band + inbox[kind, begin_in + m * wide : begin_in + (m + 1) * wide, :]
            partial[begin + m * wide : begin + (m + 1) * wide, :] = band
            spot = STARTS[piece] % SUBLANES + m
            edge = jnp.where(lane == spot, pltpu.roll(b, spot, axis=1) if spot else b, edge)
        edge = edge.T[0:SUBLANES]
        for kind in kinds:
            edge = edge + inbox[kind, begin_in + size * wide : begin_in + size * wide + SUBLANES, :]
        partial[begin + size * wide : begin + size * wide + SUBLANES, :] = edge

    sent = []

    def go(copy):
        copy.start()
        sent.append(copy)

    def pass_over(unit):
        piece, _ = UNITS[unit]
        return pltpu.make_async_remote_copy(
            src_ref=partial.at[unit_rows(unit)],
            dst_ref=across.at[piece_rows(piece)],
            send_sem=over_send.at[piece],
            recv_sem=over_recv.at[piece],
            device_id=place(low_mate, high_mate),
            device_id_type=MESH,
        )

    def collect(which, unit):
        keep(which, unit).wait()
        to_mate(which, unit).wait_recv()
        for sender in range(2):
            from_other(which, unit, sender).wait_recv()

    def process(unit):
        collect(1, unit)
        extend(unit, True).wait_recv()
        extend(unit, False).wait_recv()
        piece, hop = UNITS[unit]
        rising = RISING[piece]
        toward = up if rising else down
        if hop == 2:
            correlate(unit, ())
            go(ring(FAR, unit, toward))
        elif hop == 0:
            ring(SUM, unit, toward).wait_recv()
            ring(NEAR, unit, toward).wait_recv()
            correlate(unit, (SUM, NEAR))

            @pl.when(jnp.logical_not(sums_here))
            def _():
                pass_over(unit).start()
        elif (hop == 1) == rising:
            ring(FAR, unit, toward).wait_recv()
            correlate(unit, (FAR,))
            go(ring(SUM, unit, toward))
        else:
            correlate(unit, ())
            go(ring(NEAR, unit, down if rising else up))

    def bring_home(piece, owner):
        rows = pl.ds(STARTS[piece], SIZES[piece])
        return pltpu.make_async_remote_copy(
            src_ref=total.at[rows, pl.ds((QUAD - 1 - owner) * cells, cells)],
            dst_ref=landed.at[core, rows],
            send_sem=home_send.at[owner, piece],
            recv_sem=home_recv.at[core, piece],
            device_id=place(quad + owner, shot),
            device_id_type=MESH,
        )

    def bring_edge(owner):
        return pltpu.make_async_remote_copy(
            src_ref=total_edge,
            dst_ref=landed_edge.at[core],
            send_sem=home_send.at[owner, len(SIZES)],
            recv_sem=home_recv.at[core, len(SIZES)],
            device_id=place(quad + owner, shot),
            device_id_type=MESH,
        )

    def finish(piece):
        unit = UNITS.index((piece, 0))
        size = SIZES[piece]
        begin, begin_in = FIRST[unit] * wide + unit * SUBLANES, STARTS[piece] * wide + piece * SUBLANES

        @pl.when(sums_here)
        def _():
            pass_over(unit).wait_recv()
            for m in range(size):
                total[STARTS[piece] + m] = (
                    partial[begin + m * wide : begin + (m + 1) * wide, :]
                    + across[begin_in + m * wide : begin_in + (m + 1) * wide, :]
                )
            edge = (
                partial[begin + size * wide : begin + size * wide + SUBLANES, :]
                + across[begin_in + size * wide : begin_in + size * wide + SUBLANES, :]
            )
            total_edge[piece] = edge
            for owner in (2, 3, 0, 1):

                @pl.when(place_in_quad != owner)
                def _(owner=owner):
                    bring_home(piece, owner).start()
                    if piece == len(SIZES) - 1:
                        bring_edge(owner).start()

                @pl.when(place_in_quad == owner)
                def _(owner=owner):
                    rows = slice(STARTS[piece], STARTS[piece] + size)
                    cut = slice((QUAD - 1 - owner) * cells, (QUAD - owner) * cells)
                    landed[core, rows] = total[rows, cut]
                    landed_edge[core, piece] = edge

    def forward(unit):
        collect(0, unit)
        go(extend(unit, True))
        go(extend(unit, False))

    for which in range(2):
        for tile in range(2):
            relayout(which, tile)
            if which == 0 and tile == 0:
                pl.semaphore_wait(barrier, len(peers))
            for unit in range(AHEAD):
                go(to_other(which, unit, tile))
        for unit in range(AHEAD):
            go(to_mate(which, unit))
            keep(which, unit).start()
    for unit in range(AHEAD, len(UNITS)):
        for which in range(2):
            for tile in range(2):
                go(to_other(which, unit, tile))
    for unit in range(AHEAD, len(UNITS)):
        for which in range(2):
            go(to_mate(which, unit))
            keep(which, unit).start()

    forward(0)
    for unit in range(len(UNITS)):
        if unit + 1 < len(UNITS):
            forward(unit + 1)
        if UNITS[unit] == (2, 0):
            finish(0)
        if UNITS[unit] == (4, 0):
            finish(1)
        process(unit)
    for piece in range(2, len(SIZES)):
        finish(piece)

    groups = ((0, 1), (2, 3, 4))
    for summer in range(2):
        for group, pieces in enumerate(groups):
            elsewhere = place_in_quad != (QUAD - 1) * summer

            @pl.when(elsewhere)
            def _(summer=summer, pieces=pieces):
                for piece in pieces:
                    pltpu.make_async_remote_copy(
                        src_ref=total.at[pl.ds(STARTS[piece], SIZES[piece]), pl.ds(0, cells)],
                        dst_ref=landed.at[summer, pl.ds(STARTS[piece], SIZES[piece])],
                        send_sem=home_send.at[0, piece],
                        recv_sem=home_recv.at[summer, piece],
                        device_id=place(low_mate, shot),
                        device_id_type=MESH,
                    ).wait_recv()

            rows = pl.ds(summer * share + group * SUBLANES, SUBLANES)
            for i in range(cells):
                out[i, rows, 0:LANES] = landed[
                    summer, group * SUBLANES : (group + 1) * SUBLANES, cells - 1 - i, :
                ]
    for summer in range(2):

        @pl.when(place_in_quad != (QUAD - 1) * summer)
        def _(summer=summer):
            pltpu.make_async_remote_copy(
                src_ref=total_edge,
                dst_ref=landed_edge.at[summer],
                send_sem=home_send.at[0, len(SIZES)],
                recv_sem=home_recv.at[summer, len(SIZES)],
                device_id=place(low_mate, shot),
                device_id_type=MESH,
            ).wait_recv()

        for group, pieces in enumerate(groups):
            edge = sum(landed_edge[summer, piece] for piece in pieces)
            edge = pltpu.roll(edge, (place_in_quad + 1) * cells, axis=1)
            rows = pl.ds(summer * share + group * SUBLANES, SUBLANES)
            for i in range(cells):
                back = cells - 1 - i
                out[i, rows, LANES : LANES + 1] = edge[:, back : back + 1]

    for copy in sent:
        copy.wait_send()

    @pl.when(jnp.logical_not(sums_here))
    def _():
        for piece in range(len(SIZES)):
            pass_over(UNITS.index((piece, 0))).wait_send()

    @pl.when(sums_here)
    def _():
        for owner in range(QUAD):

            @pl.when(place_in_quad != owner)
            def _(owner=owner):
                for piece in range(len(SIZES)):
                    bring_home(piece, owner).wait_send()
                bring_edge(owner).wait_send()


def on_device(source, receiver):
    shots, cells, times, cross = source.shape
    all_shots = shots * lax.axis_size("shot")
    block = cross // 8
    share = sum(SIZES)
    wide = QUAD * cells
    scale = 1.0 / (times * all_shots) ** 0.5
    lags = wide + 1
    units, pieces = len(UNITS), len(SIZES)
    image = pl.pallas_call(
        kernel,
        out_shape=jax.ShapeDtypeStruct((cells, block, lags), F32),
        in_specs=[pl.BlockSpec(memory_space=pl.ANY)] * 2,
        out_specs=pl.BlockSpec(memory_space=pltpu.VMEM),
        scratch_shapes=[
            pltpu.VMEM((2, 2, shots, cells, times, LANES), BF16),
            pltpu.VMEM((cells * LANES, LANES), F32),
            pltpu.VMEM((2, cross, cells, LANES), BF16),
            pltpu.VMEM((QUAD, 4 * share, cells, LANES), BF16),
            pltpu.VMEM((2 * QUAD, 4 * share, cells, LANES), BF16),
            pltpu.VMEM((4 * share * wide + units * SUBLANES, LANES), F32),
            pltpu.VMEM((3, share * wide + pieces * SUBLANES, LANES), F32),
            pltpu.VMEM((share * wide + pieces * SUBLANES, LANES), F32),
            pltpu.VMEM((share, wide, LANES), F32),
            pltpu.VMEM((pieces, SUBLANES, LANES), F32),
            pltpu.VMEM((2, share, cells, LANES), F32),
            pltpu.VMEM((2, pieces, SUBLANES, LANES), F32),
            pltpu.SemaphoreType.DMA((2, 2)),
            pltpu.SemaphoreType.DMA((2, units)),
            pltpu.SemaphoreType.DMA((2, 3, units)),
            pltpu.SemaphoreType.DMA((2, 3, units)),
            pltpu.SemaphoreType.DMA((2, units)),
            pltpu.SemaphoreType.DMA((2, units)),
            pltpu.SemaphoreType.DMA((3, pieces)),
            pltpu.SemaphoreType.DMA((3, pieces)),
            pltpu.SemaphoreType.DMA((pieces,)),
            pltpu.SemaphoreType.DMA((pieces,)),
            pltpu.SemaphoreType.DMA((QUAD, pieces + 1)),
            pltpu.SemaphoreType.DMA((2, pieces + 1)),
        ],
        compiler_params=pltpu.CompilerParams(collective_id=0, has_side_effects=True, vmem_limit_bytes=60 * 2**20),
    )(source, receiver)
    return jnp.transpose(image * scale, (2, 0, 1))


def solution(mesh):
    placed = (P("shot", "inline", None, None), P("shot", "inline", None, None))
    return jax.shard_map(
        on_device, mesh=mesh, in_specs=placed, out_specs=P(None, "inline", "shot"), check_vma=False
    )
```

```python
import functools

import jax
import jax.numpy as jnp
from jax import lax
from jax.experimental import pallas as pl
from jax.experimental.pallas import tpu as pltpu
from jax.sharding import PartitionSpec as P

MESH = pl.DeviceIdType.MESH
F32 = jnp.float32
BF16 = jnp.bfloat16
LANES = 128
SUBLANES = 8
RINGS = 4
QUAD = 4
SIZES = (4, 4, 4, 2, 2)
STARTS = (0, 4, 8, 12, 14)
RISING = (True, False, True, False, False)
UNITS = (
    (0, 2), (1, 2), (2, 2), (3, 2), (4, 2), (0, 1), (1, 3), (1, 1), (0, 3), (2, 1),
    (2, 3), (3, 3), (3, 1), (0, 0), (4, 3), (4, 1), (1, 0), (2, 0), (3, 0), (4, 0),
)
GROUPS = ((0, 2), (2, 5))
FIRST = [sum(SIZES[piece] for piece, _ in UNITS[:unit]) for unit in range(len(UNITS))]
FAR, SUM, NEAR = range(3)
AHEAD = 2
LEAD = 3
SPLIT = len(UNITS) - 3


def kernel(
    scale, source, receiver, out,
    raw, turned, own, held, beside, partial, inbox, across, total, total_edge, landed, landed_edge,
    raw_sem, own_sem, ship_send, ship_recv, along_send, along_recv, ring_send, ring_recv,
    over_send, over_recv, home_send, home_recv,
):
    shots, cells, times, _ = source.shape
    share = sum(SIZES)
    wide = QUAD * cells
    owners = lax.axis_size("inline")
    me, shot = lax.axis_index("inline"), lax.axis_index("shot")
    core, low, x, high = me % 2, (me // 2) % 2, shot % RINGS, shot // RINGS
    place_in_quad, z = me % QUAD, me // QUAD
    quad = z * QUAD
    core_mate = me + 1 - 2 * core
    low_mate = me + 2 - 4 * low
    above = (me + QUAD) % owners
    below = (me + owners - QUAD) % owners
    up = high * RINGS + (x + 1) % RINGS
    down = high * RINGS + (x + RINGS - 1) % RINGS
    high_mate = (1 - high) * RINGS + x
    diagonal = low_mate + 1 - 2 * core
    peers = [
        (core_mate, shot), (low_mate, shot), (diagonal, shot), (above, shot), (below, shot),
        (me, up), (me, down), (low_mate, high_mate),
    ]
    sums_here = low == core

    def place(inline, line):
        return {"inline": inline, "shot": line}

    loads = []
    tiles = [pl.multiple_of(((high + 1 + role) % 2) * LANES, LANES) for role in range(2)]
    for tile in range(2):
        for which, array in enumerate((receiver, source)):
            loads.append(
                pltpu.make_async_copy(
                    array.at[:, :, :, pl.ds(tiles[tile], LANES)], raw.at[which, tile], raw_sem.at[which, tile]
                )
            )
            loads[-1].start()

    barrier = pltpu.get_barrier_semaphore()
    for inline, line in peers:
        pl.semaphore_signal(barrier, inc=1, device_id=place(inline, line), device_id_type=MESH)

    def relayout(which, tile):
        loads[2 * tile + which].wait()

        def turn(i, carry):
            rows = jnp.concatenate([raw[which, tile, s, i] for s in range(shots)], axis=0)
            row = cells - 1 - i if which else i
            turned[pl.ds(pl.multiple_of(row * LANES, LANES), LANES), :] = rows.T.astype(F32)
            return carry

        def gather(y, carry):
            own[tiles[tile] + y, which * cells : (which + 1) * cells] = turned[pl.ds(y, cells, stride=LANES), :].astype(BF16)
            return carry

        lax.fori_loop(0, cells, turn, 0, unroll=8)
        lax.fori_loop(0, LANES, gather, 0, unroll=16)

    def rows_from(unit, half, target_core):
        piece, hop = UNITS[unit]
        start = half * LANES + ((x + hop) % RINGS) * 2 * share + target_core * share + STARTS[piece]
        return pl.ds(start, SIZES[piece])

    def rows_to(unit):
        return pl.ds(FIRST[unit], SIZES[UNITS[unit][0]])

    def ship(unit, half, target, target_core, sent_as, received_as, part=None):
        inner = pl.ds(0, 2 * cells) if part is None else pl.ds(part * cells, cells)
        column = len(UNITS) + unit - SPLIT if part else unit
        return pltpu.make_async_remote_copy(
            src_ref=own.at[rows_from(unit, half, target_core), inner],
            dst_ref=held.at[place_in_quad, rows_to(unit), inner],
            send_sem=ship_send.at[sent_as, column],
            recv_sem=ship_recv.at[received_as, column],
            device_id=place(target, shot),
            device_id_type=MESH,
        )

    def to_mate(unit):
        return ship(unit, (low + high + 1 - core) % 2, core_mate, 1 - core, 0, 0)

    def to_other(unit, role, part=None):
        target_core = (role - low) % 2
        target = quad + 2 * (1 - low) + target_core
        return ship(unit, (high + 1 + role) % 2, target, target_core, 1 + role, 1 + core, part)

    def from_other(unit, part=None):
        for sender in range(2):
            ship(unit, 0, low_mate, core, 1, 1 + sender, part).wait_recv()

    def keep(unit):
        return pltpu.make_async_copy(
            own.at[rows_from(unit, (low + high + core) % 2, core)],
            held.at[place_in_quad, rows_to(unit)],
            own_sem.at[unit],
        )

    def extend(unit, upward):
        rows = rows_to(unit)
        begin, end = (2, 0) if upward else (0, 2)
        return pltpu.make_async_remote_copy(
            src_ref=held.at[pl.ds(begin, 2), rows, pl.ds(0, cells)],
            dst_ref=beside.at[pl.ds(end, 2), rows],
            send_sem=along_send.at[int(upward), unit],
            recv_sem=along_recv.at[int(upward), unit],
            device_id=place(above if upward else below, shot),
            device_id_type=MESH,
        )

    def unit_rows(unit):
        return pl.ds(FIRST[unit] * wide + unit * SUBLANES, SIZES[UNITS[unit][0]] * wide + SUBLANES)

    def piece_rows(piece):
        return pl.ds(STARTS[piece] * wide + piece * SUBLANES, SIZES[piece] * wide + SUBLANES)

    def ring(kind, unit, line):
        piece, _ = UNITS[unit]
        return pltpu.make_async_remote_copy(
            src_ref=partial.at[unit_rows(unit)],
            dst_ref=inbox.at[kind, piece_rows(piece)],
            send_sem=ring_send.at[kind, piece],
            recv_sem=ring_recv.at[kind, piece],
            device_id=place(me, line),
            device_id_type=MESH,
        )

    lane = lax.broadcasted_iota(jnp.int32, (wide, LANES), 1)
    straight = lane <= lax.broadcasted_iota(jnp.int32, (wide, LANES), 0)

    def correlate(unit, kinds):
        piece, _ = UNITS[unit]
        size = SIZES[piece]
        begin, begin_in = FIRST[unit] * wide + unit * SUBLANES, STARTS[piece] * wide + piece * SUBLANES

        @pl.when(z == 0)
        def _():
            beside[0:2, rows_to(unit)] = jnp.zeros((2, size, cells, LANES), BF16)

        @pl.when(z == owners // QUAD - 1)
        def _():
            beside[2:4, rows_to(unit)] = jnp.zeros((2, size, cells, LANES), BF16)

        edge = jnp.zeros((wide, LANES), F32)
        for m in range(size):
            y = FIRST[unit] + m
            contract = (((1,), (1,)), ((), ()))
            rows = jnp.concatenate([held[QUAD - 1 - part, y, cells:] for part in range(QUAD)], axis=0)
            columns = [beside[0, y], beside[1, y]] + [held[part, y, :cells] for part in range(QUAD)]
            columns = jnp.concatenate(columns + [beside[2, y], beside[3, y]], axis=0)
            product = lax.dot_general(rows, columns, contract, preferred_element_type=F32)
            a = pltpu.roll(product[:, 0:LANES], 1, axis=1, stride=1, stride_axis=0)
            b = pltpu.roll(product[:, LANES:], 1, axis=1, stride=1, stride_axis=0)
            band = jnp.where(straight, a, b)
            for kind in kinds:
                band = band + inbox[kind, begin_in + m * wide : begin_in + (m + 1) * wide, :]
            partial[begin + m * wide : begin + (m + 1) * wide, :] = band
            spot = STARTS[piece] % SUBLANES + m
            edge = jnp.where(lane == spot, pltpu.roll(b, spot, axis=1) if spot else b, edge)
        edge = edge.T[0:SUBLANES]
        for kind in kinds:
            edge = edge + inbox[kind, begin_in + size * wide : begin_in + size * wide + SUBLANES, :]
        partial[begin + size * wide : begin + size * wide + SUBLANES, :] = edge

    sent = []

    def go(copy):
        copy.start()
        sent.append(copy)

    def pass_over(unit):
        piece, _ = UNITS[unit]
        return pltpu.make_async_remote_copy(
            src_ref=partial.at[unit_rows(unit)],
            dst_ref=across.at[piece_rows(piece)],
            send_sem=over_send.at[piece],
            recv_sem=over_recv.at[piece],
            device_id=place(low_mate, high_mate),
            device_id_type=MESH,
        )

    def process(unit):
        if unit >= SPLIT:
            from_other(unit, 1)
        extend(unit, True).wait_recv()
        extend(unit, False).wait_recv()
        piece, hop = UNITS[unit]
        rising = RISING[piece]
        toward = up if rising else down
        if hop == 2:
            correlate(unit, ())
            go(ring(FAR, unit, toward))
        elif hop == 0:
            ring(SUM, unit, toward).wait_recv()
            ring(NEAR, unit, toward).wait_recv()
            correlate(unit, (SUM, NEAR))

            @pl.when(jnp.logical_not(sums_here))
            def _():
                pass_over(unit).start()
        elif (hop == 1) == rising:
            ring(FAR, unit, toward).wait_recv()
            correlate(unit, (FAR,))
            go(ring(SUM, unit, toward))
        else:
            correlate(unit, ())
            go(ring(NEAR, unit, down if rising else up))

    def bring_home(piece, owner):
        rows = pl.ds(STARTS[piece], SIZES[piece])
        return pltpu.make_async_remote_copy(
            src_ref=total.at[rows, pl.ds((QUAD - 1 - owner) * cells, cells)],
            dst_ref=landed.at[core, rows],
            send_sem=home_send.at[owner, piece],
            recv_sem=home_recv.at[core, piece],
            device_id=place(quad + owner, shot),
            device_id_type=MESH,
        )

    def bring_edge(group, owner):
        rows = pl.ds(GROUPS[group][0], GROUPS[group][1] - GROUPS[group][0])
        return pltpu.make_async_remote_copy(
            src_ref=total_edge.at[rows],
            dst_ref=landed_edge.at[core, rows],
            send_sem=home_send.at[owner, len(SIZES) + group],
            recv_sem=home_recv.at[core, len(SIZES) + group],
            device_id=place(quad + owner, shot),
            device_id_type=MESH,
        )

    def finish(piece):
        unit = UNITS.index((piece, 0))
        size = SIZES[piece]
        begin, begin_in = FIRST[unit] * wide + unit * SUBLANES, STARTS[piece] * wide + piece * SUBLANES

        @pl.when(sums_here)
        def _():
            pass_over(unit).wait_recv()
            for m in range(size):
                total[STARTS[piece] + m] = (
                    partial[begin + m * wide : begin + (m + 1) * wide, :]
                    + across[begin_in + m * wide : begin_in + (m + 1) * wide, :]
                )
            edge = (
                partial[begin + size * wide : begin + size * wide + SUBLANES, :]
                + across[begin_in + size * wide : begin_in + size * wide + SUBLANES, :]
            )
            total_edge[piece] = edge
            for owner in (2, 3, 0, 1):

                @pl.when(place_in_quad != owner)
                def _(owner=owner):
                    bring_home(piece, owner).start()
                    for group, (_, stop) in enumerate(GROUPS):
                        if piece == stop - 1:
                            bring_edge(group, owner).start()

                @pl.when(place_in_quad == owner)
                def _(owner=owner):
                    rows = slice(STARTS[piece], STARTS[piece] + size)
                    cut = slice((QUAD - 1 - owner) * cells, (QUAD - owner) * cells)
                    landed[core, rows] = total[rows, cut]
                    landed_edge[core, piece] = edge

    def forward(unit):
        keep(unit).wait()
        to_mate(unit).wait_recv()
        from_other(unit, 0 if unit >= SPLIT else None)
        go(extend(unit, True))
        go(extend(unit, False))

    def land(group):
        pieces = range(*GROUPS[group])
        for summer in range(2):

            @pl.when(place_in_quad != (QUAD - 1) * summer)
            def _(summer=summer):
                for piece in pieces:
                    rows = pl.ds(STARTS[piece], SIZES[piece])
                    pltpu.make_async_remote_copy(
                        src_ref=total.at[rows, pl.ds(0, cells)],
                        dst_ref=landed.at[summer, rows],
                        send_sem=home_send.at[0, piece],
                        recv_sem=home_recv.at[summer, piece],
                        device_id=place(low_mate, shot),
                        device_id_type=MESH,
                    ).wait_recv()
                rows = pl.ds(GROUPS[group][0], GROUPS[group][1] - GROUPS[group][0])
                pltpu.make_async_remote_copy(
                    src_ref=total_edge.at[rows],
                    dst_ref=landed_edge.at[summer, rows],
                    send_sem=home_send.at[0, len(SIZES) + group],
                    recv_sem=home_recv.at[summer, len(SIZES) + group],
                    device_id=place(low_mate, shot),
                    device_id_type=MESH,
                ).wait_recv()

            edge = sum(landed_edge[summer, piece] for piece in pieces) * scale
            edge = pltpu.roll(edge, (place_in_quad + 1) * cells, axis=1)
            rows = pl.ds(summer * share + group * SUBLANES, SUBLANES)
            for i in range(cells):
                back = cells - 1 - i
                strip = landed[summer, group * SUBLANES : (group + 1) * SUBLANES, back, :]
                out[i, rows, 0:LANES] = strip * scale
                out[i, rows, LANES : LANES + 1] = edge[:, back : back + 1]

    queue = [[(unit, role, None) for unit in range(SPLIT)] for role in range(2)]
    for role in range(2):
        for part in range(2):
            queue[role] += [(unit, role, part) for unit in range(SPLIT, len(UNITS))]
    relayout(0, 0)
    relayout(1, 0)
    pl.semaphore_wait(barrier, len(peers))
    for item in queue[0][:LEAD]:
        go(to_other(*item))
    relayout(0, 1)
    relayout(1, 1)
    for unit in range(AHEAD):
        go(to_mate(unit))
        keep(unit).start()
    for index in range(len(queue[0]) + LEAD):
        if index >= LEAD:
            go(to_other(*queue[1][index - LEAD]))
        if LEAD <= index < len(queue[0]):
            go(to_other(*queue[0][index]))
        if AHEAD <= index - LEAD + AHEAD < len(UNITS):
            go(to_mate(index - LEAD + AHEAD))
            keep(index - LEAD + AHEAD).start()

    forward(0)
    for unit in range(len(UNITS)):
        if unit + 1 < SPLIT:
            forward(unit + 1)
        if UNITS[unit] == (1, 0):
            finish(0)
        if UNITS[unit] == (4, 0):
            finish(1)
        process(unit)
        if unit + 1 == SPLIT:
            for later in range(SPLIT, len(UNITS)):
                forward(later)
    finish(2)
    land(0)
    finish(3)
    finish(4)
    land(1)

    for copy in sent:
        copy.wait_send()

    @pl.when(jnp.logical_not(sums_here))
    def _():
        for piece in range(len(SIZES)):
            pass_over(UNITS.index((piece, 0))).wait_send()

    @pl.when(sums_here)
    def _():
        for owner in range(QUAD):

            @pl.when(place_in_quad != owner)
            def _(owner=owner):
                for piece in range(len(SIZES)):
                    bring_home(piece, owner).wait_send()
                for group in range(len(GROUPS)):
                    bring_edge(group, owner).wait_send()


def on_device(source, receiver):
    shots, cells, times, cross = source.shape
    all_shots = shots * lax.axis_size("shot")
    block = cross // 8
    share = sum(SIZES)
    wide = QUAD * cells
    scale = 1.0 / (times * all_shots) ** 0.5
    lags = wide + 1
    units, pieces = len(UNITS), len(SIZES)
    image = pl.pallas_call(
        functools.partial(kernel, scale),
        out_shape=jax.ShapeDtypeStruct((cells, block, lags), F32),
        in_specs=[pl.BlockSpec(memory_space=pl.ANY)] * 2,
        out_specs=pl.BlockSpec(memory_space=pltpu.VMEM),
        scratch_shapes=[
            pltpu.VMEM((2, 2, shots, cells, times, LANES), BF16),
            pltpu.VMEM((cells * LANES, LANES), F32),
            pltpu.VMEM((cross, 2 * cells, LANES), BF16),
            pltpu.VMEM((QUAD, 4 * share, 2 * cells, LANES), BF16),
            pltpu.VMEM((QUAD, 4 * share, cells, LANES), BF16),
            pltpu.VMEM((4 * share * wide + units * SUBLANES, LANES), F32),
            pltpu.VMEM((3, share * wide + pieces * SUBLANES, LANES), F32),
            pltpu.VMEM((share * wide + pieces * SUBLANES, LANES), F32),
            pltpu.VMEM((share, wide, LANES), F32),
            pltpu.VMEM((pieces, SUBLANES, LANES), F32),
            pltpu.VMEM((2, share, cells, LANES), F32),
            pltpu.VMEM((2, pieces, SUBLANES, LANES), F32),
            pltpu.SemaphoreType.DMA((2, 2)),
            pltpu.SemaphoreType.DMA((units,)),
            pltpu.SemaphoreType.DMA((3, 2 * units - SPLIT)),
            pltpu.SemaphoreType.DMA((3, 2 * units - SPLIT)),
            pltpu.SemaphoreType.DMA((2, units)),
            pltpu.SemaphoreType.DMA((2, units)),
            pltpu.SemaphoreType.DMA((3, pieces)),
            pltpu.SemaphoreType.DMA((3, pieces)),
            pltpu.SemaphoreType.DMA((pieces,)),
            pltpu.SemaphoreType.DMA((pieces,)),
            pltpu.SemaphoreType.DMA((QUAD, pieces + len(GROUPS))),
            pltpu.SemaphoreType.DMA((2, pieces + len(GROUPS))),
        ],
        compiler_params=pltpu.CompilerParams(collective_id=0, has_side_effects=True, vmem_limit_bytes=60 * 2**20),
    )(source, receiver)
    return jnp.transpose(image, (2, 0, 1))


def solution(mesh):
    placed = (P("shot", "inline", None, None), P("shot", "inline", None, None))
    return jax.shard_map(
        on_device, mesh=mesh, in_specs=placed, out_specs=P(None, "inline", "shot"), check_vma=False
    )
```

```python
import functools

import jax
import jax.numpy as jnp
from jax import lax
from jax.experimental import pallas as pl
from jax.experimental.pallas import tpu as pltpu
from jax.sharding import PartitionSpec as P

MESH = pl.DeviceIdType.MESH
F32 = jnp.float32
BF16 = jnp.bfloat16
LANES = 128
SUBLANES = 8
RINGS = 4
QUAD = 4
SIZES = (4, 4, 4, 2, 2)
STARTS = (0, 4, 8, 12, 14)
RISING = (True, False, True, False, False)
UNITS = (
    (0, 2), (1, 2), (2, 2), (3, 2), (4, 2), (0, 1), (1, 3), (1, 1), (0, 3), (2, 1),
    (2, 3), (3, 3), (3, 1), (0, 0), (4, 3), (4, 1), (1, 0), (2, 0), (3, 0), (4, 0),
)
GROUPS = ((0, 2), (2, 5))
FIRST = [sum(SIZES[piece] for piece, _ in UNITS[:unit]) for unit in range(len(UNITS))]
FAR, SUM, NEAR = range(3)
AHEAD = 2
LEAD = 3
SPLIT = len(UNITS) - 3


def kernel(
    scale, source, receiver, out,
    raw, turned, own, held, beside, partial, inbox, across, total, total_edge, landed, landed_edge,
    raw_sem, own_sem, ship_send, ship_recv, along_send, along_recv, ring_send, ring_recv,
    over_send, over_recv, home_send, home_recv,
):
    shots, cells, times, _ = source.shape
    share = sum(SIZES)
    wide = QUAD * cells
    owners = lax.axis_size("inline")
    me, shot = lax.axis_index("inline"), lax.axis_index("shot")
    core, low, x, high = me % 2, (me // 2) % 2, shot % RINGS, shot // RINGS
    place_in_quad, z = me % QUAD, me // QUAD
    quad = z * QUAD
    core_mate = me + 1 - 2 * core
    low_mate = me + 2 - 4 * low
    above = (me + QUAD) % owners
    below = (me + owners - QUAD) % owners
    up = high * RINGS + (x + 1) % RINGS
    down = high * RINGS + (x + RINGS - 1) % RINGS
    high_mate = (1 - high) * RINGS + x
    diagonal = low_mate + 1 - 2 * core
    peers = [
        (core_mate, shot), (low_mate, shot), (diagonal, shot), (me, up), (me, down), (low_mate, high_mate),
    ]
    last = owners // QUAD - 1
    sums_here = low == core

    def place(inline, line):
        return {"inline": inline, "shot": line}

    loads = []
    tiles = [pl.multiple_of(((high + 1 + role) % 2) * LANES, LANES) for role in range(2)]
    for tile in range(2):
        for which, array in enumerate((receiver, source)):
            loads.append(
                pltpu.make_async_copy(
                    array.at[:, :, :, pl.ds(tiles[tile], LANES)], raw.at[which, tile], raw_sem.at[which, tile]
                )
            )
            loads[-1].start()

    barrier = pltpu.get_barrier_semaphore()
    for inline, line in peers:
        pl.semaphore_signal(barrier, inc=1, device_id=place(inline, line), device_id_type=MESH)
    for there, inline in ((z < last, above), (z > 0, below)):

        @pl.when(there)
        def _(inline=inline):
            pl.semaphore_signal(barrier, inc=1, device_id=place(inline, shot), device_id_type=MESH)

    def relayout(which, tile):
        loads[2 * tile + which].wait()

        def turn(i, carry):
            rows = jnp.concatenate([raw[which, tile, s, i] for s in range(shots)], axis=0)
            row = cells - 1 - i if which else i
            turned[pl.ds(pl.multiple_of(row * LANES, LANES), LANES), :] = rows.T.astype(F32)
            return carry

        def gather(y, carry):
            own[tiles[tile] + y, which * cells : (which + 1) * cells] = turned[pl.ds(y, cells, stride=LANES), :].astype(BF16)
            return carry

        lax.fori_loop(0, cells, turn, 0, unroll=8)
        lax.fori_loop(0, LANES, gather, 0, unroll=16)

    def rows_from(unit, half, target_core):
        piece, hop = UNITS[unit]
        start = half * LANES + ((x + hop) % RINGS) * 2 * share + target_core * share + STARTS[piece]
        return pl.ds(start, SIZES[piece])

    def rows_to(unit):
        return pl.ds(FIRST[unit], SIZES[UNITS[unit][0]])

    def ship(unit, half, target, target_core, sent_as, received_as, part=None):
        inner = pl.ds(0, 2 * cells) if part is None else pl.ds(part * cells, cells)
        column = len(UNITS) + unit - SPLIT if part else unit
        return pltpu.make_async_remote_copy(
            src_ref=own.at[rows_from(unit, half, target_core), inner],
            dst_ref=held.at[place_in_quad, rows_to(unit), inner],
            send_sem=ship_send.at[sent_as, column],
            recv_sem=ship_recv.at[received_as, column],
            device_id=place(target, shot),
            device_id_type=MESH,
        )

    def to_mate(unit):
        return ship(unit, (low + high + 1 - core) % 2, core_mate, 1 - core, 0, 0)

    def to_other(unit, role, part=None):
        target_core = (role - low) % 2
        target = quad + 2 * (1 - low) + target_core
        return ship(unit, (high + 1 + role) % 2, target, target_core, 1 + role, 1 + core, part)

    def from_other(unit, part=None):
        for sender in range(2):
            ship(unit, 0, low_mate, core, 1, 1 + sender, part).wait_recv()

    def keep(unit):
        return pltpu.make_async_copy(
            own.at[rows_from(unit, (low + high + core) % 2, core)],
            held.at[place_in_quad, rows_to(unit)],
            own_sem.at[unit],
        )

    def extend(unit, upward):
        rows = rows_to(unit)
        begin, end = (2, 0) if upward else (0, 2)
        return pltpu.make_async_remote_copy(
            src_ref=held.at[pl.ds(begin, 2), rows, pl.ds(0, cells)],
            dst_ref=beside.at[pl.ds(end, 2), rows],
            send_sem=along_send.at[int(upward), unit],
            recv_sem=along_recv.at[int(upward), unit],
            device_id=place(above if upward else below, shot),
            device_id_type=MESH,
        )

    def unit_rows(unit):
        return pl.ds(FIRST[unit] * wide + unit * SUBLANES, SIZES[UNITS[unit][0]] * wide + SUBLANES)

    def piece_rows(piece):
        return pl.ds(STARTS[piece] * wide + piece * SUBLANES, SIZES[piece] * wide + SUBLANES)

    def ring(kind, unit, line):
        piece, _ = UNITS[unit]
        return pltpu.make_async_remote_copy(
            src_ref=partial.at[unit_rows(unit)],
            dst_ref=inbox.at[kind, piece_rows(piece)],
            send_sem=ring_send.at[kind, piece],
            recv_sem=ring_recv.at[kind, piece],
            device_id=place(me, line),
            device_id_type=MESH,
        )

    lane = lax.broadcasted_iota(jnp.int32, (wide, LANES), 1)
    straight = lane <= lax.broadcasted_iota(jnp.int32, (wide, LANES), 0)

    def correlate(unit, kinds):
        piece, _ = UNITS[unit]
        size = SIZES[piece]
        begin, begin_in = FIRST[unit] * wide + unit * SUBLANES, STARTS[piece] * wide + piece * SUBLANES

        edge = jnp.zeros((wide, LANES), F32)
        for m in range(size):
            y = FIRST[unit] + m
            contract = (((1,), (1,)), ((), ()))
            rows = jnp.concatenate([held[QUAD - 1 - part, y, cells:] for part in range(QUAD)], axis=0)
            columns = [beside[0, y], beside[1, y]] + [held[part, y, :cells] for part in range(QUAD)]
            columns = jnp.concatenate(columns + [beside[2, y], beside[3, y]], axis=0)
            product = lax.dot_general(rows, columns, contract, preferred_element_type=F32)
            a = pltpu.roll(product[:, 0:LANES], 1, axis=1, stride=1, stride_axis=0)
            b = pltpu.roll(product[:, LANES:], 1, axis=1, stride=1, stride_axis=0)
            band = jnp.where(straight, a, b)
            for kind in kinds:
                band = band + inbox[kind, begin_in + m * wide : begin_in + (m + 1) * wide, :]
            partial[begin + m * wide : begin + (m + 1) * wide, :] = band
            spot = STARTS[piece] % SUBLANES + m
            edge = jnp.where(lane == spot, pltpu.roll(b, spot, axis=1) if spot else b, edge)
        edge = edge.T[0:SUBLANES]
        for kind in kinds:
            edge = edge + inbox[kind, begin_in + size * wide : begin_in + size * wide + SUBLANES, :]
        partial[begin + size * wide : begin + size * wide + SUBLANES, :] = edge

    sent = []

    def go(copy):
        copy.start()
        sent.append(copy)

    def pass_over(unit):
        piece, _ = UNITS[unit]
        return pltpu.make_async_remote_copy(
            src_ref=partial.at[unit_rows(unit)],
            dst_ref=across.at[piece_rows(piece)],
            send_sem=over_send.at[piece],
            recv_sem=over_recv.at[piece],
            device_id=place(low_mate, high_mate),
            device_id_type=MESH,
        )

    def process(unit):
        if unit >= SPLIT:
            from_other(unit, 1)

        @pl.when(z > 0)
        def _():
            extend(unit, True).wait_recv()

        @pl.when(z < last)
        def _():
            extend(unit, False).wait_recv()

        piece, hop = UNITS[unit]
        rising = RISING[piece]
        toward = up if rising else down
        if hop == 2:
            correlate(unit, ())
            go(ring(FAR, unit, toward))
        elif hop == 0:
            ring(SUM, unit, toward).wait_recv()
            ring(NEAR, unit, toward).wait_recv()
            correlate(unit, (SUM, NEAR))

            @pl.when(jnp.logical_not(sums_here))
            def _():
                pass_over(unit).start()
        elif (hop == 1) == rising:
            ring(FAR, unit, toward).wait_recv()
            correlate(unit, (FAR,))
            go(ring(SUM, unit, toward))
        else:
            correlate(unit, ())
            go(ring(NEAR, unit, down if rising else up))

    def bring_home(piece, owner):
        rows = pl.ds(STARTS[piece], SIZES[piece])
        return pltpu.make_async_remote_copy(
            src_ref=total.at[rows, pl.ds((QUAD - 1 - owner) * cells, cells)],
            dst_ref=landed.at[core, rows],
            send_sem=home_send.at[owner, piece],
            recv_sem=home_recv.at[core, piece],
            device_id=place(quad + owner, shot),
            device_id_type=MESH,
        )

    def bring_edge(group, owner):
        rows = pl.ds(GROUPS[group][0], GROUPS[group][1] - GROUPS[group][0])
        return pltpu.make_async_remote_copy(
            src_ref=total_edge.at[rows],
            dst_ref=landed_edge.at[core, rows],
            send_sem=home_send.at[owner, len(SIZES) + group],
            recv_sem=home_recv.at[core, len(SIZES) + group],
            device_id=place(quad + owner, shot),
            device_id_type=MESH,
        )

    def finish(piece):
        unit = UNITS.index((piece, 0))
        size = SIZES[piece]
        begin, begin_in = FIRST[unit] * wide + unit * SUBLANES, STARTS[piece] * wide + piece * SUBLANES

        @pl.when(sums_here)
        def _():
            pass_over(unit).wait_recv()
            for m in range(size):
                total[STARTS[piece] + m] = (
                    partial[begin + m * wide : begin + (m + 1) * wide, :]
                    + across[begin_in + m * wide : begin_in + (m + 1) * wide, :]
                )
            edge = (
                partial[begin + size * wide : begin + size * wide + SUBLANES, :]
                + across[begin_in + size * wide : begin_in + size * wide + SUBLANES, :]
            )
            total_edge[piece] = edge
            for owner in (2, 3, 0, 1):

                @pl.when(place_in_quad != owner)
                def _(owner=owner):
                    bring_home(piece, owner).start()
                    for group, (_, stop) in enumerate(GROUPS):
                        if piece == stop - 1:
                            bring_edge(group, owner).start()

                @pl.when(place_in_quad == owner)
                def _(owner=owner):
                    rows = slice(STARTS[piece], STARTS[piece] + size)
                    cut = slice((QUAD - 1 - owner) * cells, (QUAD - owner) * cells)
                    landed[core, rows] = total[rows, cut]
                    landed_edge[core, piece] = edge

    def forward(unit):
        keep(unit).wait()
        to_mate(unit).wait_recv()
        from_other(unit, 0 if unit >= SPLIT else None)

        @pl.when(z < last)
        def _():
            extend(unit, True).start()

        @pl.when(z > 0)
        def _():
            extend(unit, False).start()


    def land(group):
        pieces = range(*GROUPS[group])
        for summer in range(2):

            @pl.when(place_in_quad != (QUAD - 1) * summer)
            def _(summer=summer):
                for piece in pieces:
                    rows = pl.ds(STARTS[piece], SIZES[piece])
                    pltpu.make_async_remote_copy(
                        src_ref=total.at[rows, pl.ds(0, cells)],
                        dst_ref=landed.at[summer, rows],
                        send_sem=home_send.at[0, piece],
                        recv_sem=home_recv.at[summer, piece],
                        device_id=place(low_mate, shot),
                        device_id_type=MESH,
                    ).wait_recv()
                rows = pl.ds(GROUPS[group][0], GROUPS[group][1] - GROUPS[group][0])
                pltpu.make_async_remote_copy(
                    src_ref=total_edge.at[rows],
                    dst_ref=landed_edge.at[summer, rows],
                    send_sem=home_send.at[0, len(SIZES) + group],
                    recv_sem=home_recv.at[summer, len(SIZES) + group],
                    device_id=place(low_mate, shot),
                    device_id_type=MESH,
                ).wait_recv()

            edge = sum(landed_edge[summer, piece] for piece in pieces) * scale
            edge = pltpu.roll(edge, (place_in_quad + 1) * cells, axis=1)
            rows = pl.ds(summer * share + group * SUBLANES, SUBLANES)
            for i in range(cells):
                back = cells - 1 - i
                strip = landed[summer, group * SUBLANES : (group + 1) * SUBLANES, back, :]
                out[i, rows, 0:LANES] = strip * scale
                out[i, rows, LANES : LANES + 1] = edge[:, back : back + 1]

    queue = [[(unit, role, None) for unit in range(SPLIT)] for role in range(2)]
    for role in range(2):
        for part in range(2):
            queue[role] += [(unit, role, part) for unit in range(SPLIT, len(UNITS))]
    relayout(0, 0)
    relayout(1, 0)
    pl.semaphore_wait(barrier, len(peers) + jnp.where(z < last, 1, 0) + jnp.where(z > 0, 1, 0))
    for item in queue[0][:LEAD]:
        go(to_other(*item))
    relayout(0, 1)
    relayout(1, 1)
    for unit in range(AHEAD):
        go(to_mate(unit))
        keep(unit).start()
    for index in range(len(queue[0]) + LEAD):
        if index >= LEAD:
            go(to_other(*queue[1][index - LEAD]))
        if LEAD <= index < len(queue[0]):
            go(to_other(*queue[0][index]))
        if AHEAD <= index - LEAD + AHEAD < len(UNITS):
            go(to_mate(index - LEAD + AHEAD))
            keep(index - LEAD + AHEAD).start()

    for missing, edge in ((z == 0, 0), (z == last, 2)):

        @pl.when(missing)
        def _(edge=edge):
            def clear(y, carry):
                beside[edge, y] = jnp.zeros((cells, LANES), BF16)
                beside[edge + 1, y] = jnp.zeros((cells, LANES), BF16)
                return carry

            lax.fori_loop(0, QUAD * share, clear, 0, unroll=4)

    forward(0)
    for unit in range(len(UNITS)):
        if unit + 1 < SPLIT:
            forward(unit + 1)
        if UNITS[unit] == (1, 0):
            finish(0)
        if UNITS[unit] == (4, 0):
            finish(1)
        process(unit)
        if unit + 1 == SPLIT:
            for later in range(SPLIT, len(UNITS)):
                forward(later)
    finish(2)
    land(0)
    finish(3)
    finish(4)
    land(1)

    for copy in sent:
        copy.wait_send()
    for there, upward in ((z < last, True), (z > 0, False)):

        @pl.when(there)
        def _(upward=upward):
            for unit in range(len(UNITS)):
                extend(unit, upward).wait_send()

    @pl.when(jnp.logical_not(sums_here))
    def _():
        for piece in range(len(SIZES)):
            pass_over(UNITS.index((piece, 0))).wait_send()

    @pl.when(sums_here)
    def _():
        for owner in range(QUAD):

            @pl.when(place_in_quad != owner)
            def _(owner=owner):
                for piece in range(len(SIZES)):
                    bring_home(piece, owner).wait_send()
                for group in range(len(GROUPS)):
                    bring_edge(group, owner).wait_send()


def on_device(source, receiver):
    shots, cells, times, cross = source.shape
    all_shots = shots * lax.axis_size("shot")
    block = cross // 8
    share = sum(SIZES)
    wide = QUAD * cells
    scale = 1.0 / (times * all_shots) ** 0.5
    lags = wide + 1
    units, pieces = len(UNITS), len(SIZES)
    image = pl.pallas_call(
        functools.partial(kernel, scale),
        out_shape=pltpu.VMEM((cells, block, lags), F32),
        in_specs=[pl.BlockSpec(memory_space=pl.ANY)] * 2,
        out_specs=pl.BlockSpec(memory_space=pltpu.VMEM),
        scratch_shapes=[
            pltpu.VMEM((2, 2, shots, cells, times, LANES), BF16),
            pltpu.VMEM((cells * LANES, LANES), F32),
            pltpu.VMEM((cross, 2 * cells, LANES), BF16),
            pltpu.VMEM((QUAD, 4 * share, 2 * cells, LANES), BF16),
            pltpu.VMEM((QUAD, 4 * share, cells, LANES), BF16),
            pltpu.VMEM((4 * share * wide + units * SUBLANES, LANES), F32),
            pltpu.VMEM((3, share * wide + pieces * SUBLANES, LANES), F32),
            pltpu.VMEM((share * wide + pieces * SUBLANES, LANES), F32),
            pltpu.VMEM((share, wide, LANES), F32),
            pltpu.VMEM((pieces, SUBLANES, LANES), F32),
            pltpu.VMEM((2, share, cells, LANES), F32),
            pltpu.VMEM((2, pieces, SUBLANES, LANES), F32),
            pltpu.SemaphoreType.DMA((2, 2)),
            pltpu.SemaphoreType.DMA((units,)),
            pltpu.SemaphoreType.DMA((3, 2 * units - SPLIT)),
            pltpu.SemaphoreType.DMA((3, 2 * units - SPLIT)),
            pltpu.SemaphoreType.DMA((2, units)),
            pltpu.SemaphoreType.DMA((2, units)),
            pltpu.SemaphoreType.DMA((3, pieces)),
            pltpu.SemaphoreType.DMA((3, pieces)),
            pltpu.SemaphoreType.DMA((pieces,)),
            pltpu.SemaphoreType.DMA((pieces,)),
            pltpu.SemaphoreType.DMA((QUAD, pieces + len(GROUPS))),
            pltpu.SemaphoreType.DMA((2, pieces + len(GROUPS))),
        ],
        compiler_params=pltpu.CompilerParams(collective_id=0, has_side_effects=True, vmem_limit_bytes=60 * 2**20),
    )(source, receiver)
    return jnp.transpose(image, (2, 0, 1))


def solution(mesh):
    placed = (P("shot", "inline", None, None), P("shot", "inline", None, None))
    return jax.shard_map(
        on_device, mesh=mesh, in_specs=placed, out_specs=P(None, "inline", "shot"), check_vma=False
    )
```

```python
import functools

import jax
import jax.numpy as jnp
from jax import lax
from jax.experimental import pallas as pl
from jax.experimental.pallas import tpu as pltpu
from jax.sharding import PartitionSpec as P

MESH = pl.DeviceIdType.MESH
F32 = jnp.float32
BF16 = jnp.bfloat16
LANES = 128
SUBLANES = 8
RINGS = 4
QUAD = 4
SIZES = (4, 4, 4, 2, 2)
STARTS = (0, 4, 8, 12, 14)
RISING = (True, False, True, False, False)
UNITS = (
    (0, 2), (1, 2), (2, 2), (3, 2), (4, 2), (0, 1), (1, 3), (1, 1), (0, 3), (2, 1),
    (2, 3), (3, 3), (3, 1), (0, 0), (4, 3), (4, 1), (1, 0), (2, 0), (3, 0), (4, 0),
)
GROUPS = ((0, 2), (2, 5))
FIRST = [sum(SIZES[piece] for piece, _ in UNITS[:unit]) for unit in range(len(UNITS))]
FAR, SUM, NEAR = range(3)
AHEAD = 2
LEAD = 3
SPLIT = len(UNITS) - 7


def kernel(
    scale, source, receiver, out,
    raw, turned, own, held, beside, partial, inbox, across, total, total_edge, landed, landed_edge,
    raw_sem, own_sem, ship_send, ship_recv, along_send, along_recv, ring_send, ring_recv,
    over_send, over_recv, home_send, home_recv,
):
    shots, cells, times, _ = source.shape
    share = sum(SIZES)
    wide = QUAD * cells
    owners = lax.axis_size("inline")
    me, shot = lax.axis_index("inline"), lax.axis_index("shot")
    core, low, x, high = me % 2, (me // 2) % 2, shot % RINGS, shot // RINGS
    place_in_quad, z = me % QUAD, me // QUAD
    quad = z * QUAD
    core_mate = me + 1 - 2 * core
    low_mate = me + 2 - 4 * low
    above = (me + QUAD) % owners
    below = (me + owners - QUAD) % owners
    up = high * RINGS + (x + 1) % RINGS
    down = high * RINGS + (x + RINGS - 1) % RINGS
    high_mate = (1 - high) * RINGS + x
    diagonal = low_mate + 1 - 2 * core
    peers = [
        (core_mate, shot), (low_mate, shot), (diagonal, shot), (me, up), (me, down), (low_mate, high_mate),
    ]
    last = owners // QUAD - 1
    sums_here = low == core

    def place(inline, line):
        return {"inline": inline, "shot": line}

    loads = []
    tiles = [pl.multiple_of(((high + 1 + role) % 2) * LANES, LANES) for role in range(2)]
    for tile in range(2):
        for which, array in enumerate((receiver, source)):
            loads.append(
                pltpu.make_async_copy(
                    array.at[:, :, :, pl.ds(tiles[tile], LANES)], raw.at[which, tile], raw_sem.at[which, tile]
                )
            )
            loads[-1].start()

    barrier = pltpu.get_barrier_semaphore()
    for inline, line in peers:
        pl.semaphore_signal(barrier, inc=1, device_id=place(inline, line), device_id_type=MESH)
    for there, inline in ((z < last, above), (z > 0, below)):

        @pl.when(there)
        def _(inline=inline):
            pl.semaphore_signal(barrier, inc=1, device_id=place(inline, shot), device_id_type=MESH)

    def relayout(which, tile):
        loads[2 * tile + which].wait()

        def turn(i, carry):
            rows = jnp.concatenate([raw[which, tile, s, i] for s in range(shots)], axis=0)
            row = cells - 1 - i if which else i
            turned[pl.ds(pl.multiple_of(row * LANES, LANES), LANES), :] = rows.T.astype(F32)
            return carry

        def gather(y, carry):
            own[tiles[tile] + y, which * cells : (which + 1) * cells] = turned[pl.ds(y, cells, stride=LANES), :].astype(BF16)
            return carry

        lax.fori_loop(0, cells, turn, 0, unroll=8)
        lax.fori_loop(0, LANES, gather, 0, unroll=16)

    def rows_from(unit, half, target_core):
        piece, hop = UNITS[unit]
        start = half * LANES + ((x + hop) % RINGS) * 2 * share + target_core * share + STARTS[piece]
        return pl.ds(start, SIZES[piece])

    def rows_to(unit):
        return pl.ds(FIRST[unit], SIZES[UNITS[unit][0]])

    def ship(unit, half, target, target_core, sent_as, received_as, part=None):
        inner = pl.ds(0, 2 * cells) if part is None else pl.ds(part * cells, cells)
        column = len(UNITS) + unit - SPLIT if part else unit
        return pltpu.make_async_remote_copy(
            src_ref=own.at[rows_from(unit, half, target_core), inner],
            dst_ref=held.at[place_in_quad, rows_to(unit), inner],
            send_sem=ship_send.at[sent_as, column],
            recv_sem=ship_recv.at[received_as, column],
            device_id=place(target, shot),
            device_id_type=MESH,
        )

    def to_mate(unit):
        return ship(unit, (low + high + 1 - core) % 2, core_mate, 1 - core, 0, 0)

    def to_other(unit, role, part=None):
        target_core = (role - low) % 2
        target = quad + 2 * (1 - low) + target_core
        return ship(unit, (high + 1 + role) % 2, target, target_core, 1 + role, 1 + core, part)

    def from_other(unit, part=None):
        for sender in range(2):
            ship(unit, 0, low_mate, core, 1, 1 + sender, part).wait_recv()

    def keep(unit):
        return pltpu.make_async_copy(
            own.at[rows_from(unit, (low + high + core) % 2, core)],
            held.at[place_in_quad, rows_to(unit)],
            own_sem.at[unit],
        )

    def extend(unit, upward):
        rows = rows_to(unit)
        begin, end = (2, 0) if upward else (0, 2)
        return pltpu.make_async_remote_copy(
            src_ref=held.at[pl.ds(begin, 2), rows, pl.ds(0, cells)],
            dst_ref=beside.at[pl.ds(end, 2), rows],
            send_sem=along_send.at[int(upward), unit],
            recv_sem=along_recv.at[int(upward), unit],
            device_id=place(above if upward else below, shot),
            device_id_type=MESH,
        )

    def unit_rows(unit):
        return pl.ds(FIRST[unit] * wide + unit * SUBLANES, SIZES[UNITS[unit][0]] * wide + SUBLANES)

    def piece_rows(piece):
        return pl.ds(STARTS[piece] * wide + piece * SUBLANES, SIZES[piece] * wide + SUBLANES)

    def ring(kind, unit, line):
        piece, _ = UNITS[unit]
        return pltpu.make_async_remote_copy(
            src_ref=partial.at[unit_rows(unit)],
            dst_ref=inbox.at[kind, piece_rows(piece)],
            send_sem=ring_send.at[kind, piece],
            recv_sem=ring_recv.at[kind, piece],
            device_id=place(me, line),
            device_id_type=MESH,
        )

    lane = lax.broadcasted_iota(jnp.int32, (wide, LANES), 1)
    straight = lane <= lax.broadcasted_iota(jnp.int32, (wide, LANES), 0)

    def correlate(unit, kinds):
        piece, _ = UNITS[unit]
        size = SIZES[piece]
        begin, begin_in = FIRST[unit] * wide + unit * SUBLANES, STARTS[piece] * wide + piece * SUBLANES

        edge = jnp.zeros((wide, LANES), F32)
        for m in range(size):
            y = FIRST[unit] + m
            contract = (((1,), (1,)), ((), ()))
            rows = jnp.concatenate([held[QUAD - 1 - part, y, cells:] for part in range(QUAD)], axis=0)
            columns = [beside[0, y], beside[1, y]] + [held[part, y, :cells] for part in range(QUAD)]
            columns = jnp.concatenate(columns + [beside[2, y], beside[3, y]], axis=0)
            product = lax.dot_general(rows, columns, contract, preferred_element_type=F32)
            a = pltpu.roll(product[:, 0:LANES], 1, axis=1, stride=1, stride_axis=0)
            b = pltpu.roll(product[:, LANES:], 1, axis=1, stride=1, stride_axis=0)
            band = jnp.where(straight, a, b)
            for kind in kinds:
                band = band + inbox[kind, begin_in + m * wide : begin_in + (m + 1) * wide, :]
            partial[begin + m * wide : begin + (m + 1) * wide, :] = band
            spot = STARTS[piece] % SUBLANES + m
            edge = jnp.where(lane == spot, pltpu.roll(b, spot, axis=1) if spot else b, edge)
        edge = edge.T[0:SUBLANES]
        for kind in kinds:
            edge = edge + inbox[kind, begin_in + size * wide : begin_in + size * wide + SUBLANES, :]
        partial[begin + size * wide : begin + size * wide + SUBLANES, :] = edge

    sent = []

    def go(copy):
        copy.start()
        sent.append(copy)

    def pass_over(unit):
        piece, _ = UNITS[unit]
        return pltpu.make_async_remote_copy(
            src_ref=partial.at[unit_rows(unit)],
            dst_ref=across.at[piece_rows(piece)],
            send_sem=over_send.at[piece],
            recv_sem=over_recv.at[piece],
            device_id=place(low_mate, high_mate),
            device_id_type=MESH,
        )

    def process(unit):
        if unit >= SPLIT:
            from_other(unit, 1)

        @pl.when(z > 0)
        def _():
            extend(unit, True).wait_recv()

        @pl.when(z < last)
        def _():
            extend(unit, False).wait_recv()

        piece, hop = UNITS[unit]
        rising = RISING[piece]
        toward = up if rising else down
        if hop == 2:
            correlate(unit, ())
            go(ring(FAR, unit, toward))
        elif hop == 0:
            ring(SUM, unit, toward).wait_recv()
            ring(NEAR, unit, toward).wait_recv()
            correlate(unit, (SUM, NEAR))

            @pl.when(jnp.logical_not(sums_here))
            def _():
                pass_over(unit).start()
        elif (hop == 1) == rising:
            ring(FAR, unit, toward).wait_recv()
            correlate(unit, (FAR,))
            go(ring(SUM, unit, toward))
        else:
            correlate(unit, ())
            go(ring(NEAR, unit, down if rising else up))

    def bring_home(piece, owner):
        rows = pl.ds(STARTS[piece], SIZES[piece])
        return pltpu.make_async_remote_copy(
            src_ref=total.at[rows, pl.ds((QUAD - 1 - owner) * cells, cells)],
            dst_ref=landed.at[core, rows],
            send_sem=home_send.at[owner, piece],
            recv_sem=home_recv.at[core, piece],
            device_id=place(quad + owner, shot),
            device_id_type=MESH,
        )

    def bring_edge(group, owner):
        rows = pl.ds(GROUPS[group][0], GROUPS[group][1] - GROUPS[group][0])
        return pltpu.make_async_remote_copy(
            src_ref=total_edge.at[rows],
            dst_ref=landed_edge.at[core, rows],
            send_sem=home_send.at[owner, len(SIZES) + group],
            recv_sem=home_recv.at[core, len(SIZES) + group],
            device_id=place(quad + owner, shot),
            device_id_type=MESH,
        )

    def finish(piece):
        unit = UNITS.index((piece, 0))
        size = SIZES[piece]
        begin, begin_in = FIRST[unit] * wide + unit * SUBLANES, STARTS[piece] * wide + piece * SUBLANES

        @pl.when(sums_here)
        def _():
            pass_over(unit).wait_recv()
            for m in range(size):
                total[STARTS[piece] + m] = (
                    partial[begin + m * wide : begin + (m + 1) * wide, :]
                    + across[begin_in + m * wide : begin_in + (m + 1) * wide, :]
                )
            edge = (
                partial[begin + size * wide : begin + size * wide + SUBLANES, :]
                + across[begin_in + size * wide : begin_in + size * wide + SUBLANES, :]
            )
            total_edge[piece] = edge
            for owner in (2, 3, 0, 1):

                @pl.when(place_in_quad != owner)
                def _(owner=owner):
                    bring_home(piece, owner).start()
                    for group, (_, stop) in enumerate(GROUPS):
                        if piece == stop - 1:
                            bring_edge(group, owner).start()

                @pl.when(place_in_quad == owner)
                def _(owner=owner):
                    rows = slice(STARTS[piece], STARTS[piece] + size)
                    cut = slice((QUAD - 1 - owner) * cells, (QUAD - owner) * cells)
                    landed[core, rows] = total[rows, cut]
                    landed_edge[core, piece] = edge

    def forward(unit):
        keep(unit).wait()
        to_mate(unit).wait_recv()
        from_other(unit, 0 if unit >= SPLIT else None)

        @pl.when(z < last)
        def _():
            extend(unit, True).start()

        @pl.when(z > 0)
        def _():
            extend(unit, False).start()


    def land(group):
        pieces = range(*GROUPS[group])
        for summer in range(2):

            @pl.when(place_in_quad != (QUAD - 1) * summer)
            def _(summer=summer):
                for piece in pieces:
                    rows = pl.ds(STARTS[piece], SIZES[piece])
                    pltpu.make_async_remote_copy(
                        src_ref=total.at[rows, pl.ds(0, cells)],
                        dst_ref=landed.at[summer, rows],
                        send_sem=home_send.at[0, piece],
                        recv_sem=home_recv.at[summer, piece],
                        device_id=place(low_mate, shot),
                        device_id_type=MESH,
                    ).wait_recv()
                rows = pl.ds(GROUPS[group][0], GROUPS[group][1] - GROUPS[group][0])
                pltpu.make_async_remote_copy(
                    src_ref=total_edge.at[rows],
                    dst_ref=landed_edge.at[summer, rows],
                    send_sem=home_send.at[0, len(SIZES) + group],
                    recv_sem=home_recv.at[summer, len(SIZES) + group],
                    device_id=place(low_mate, shot),
                    device_id_type=MESH,
                ).wait_recv()

            edge = sum(landed_edge[summer, piece] for piece in pieces) * scale
            edge = pltpu.roll(edge, (place_in_quad + 1) * cells, axis=1)
            rows = pl.ds(summer * share + group * SUBLANES, SUBLANES)
            for i in range(cells):
                back = cells - 1 - i
                strip = landed[summer, group * SUBLANES : (group + 1) * SUBLANES, back, :]
                out[i, rows, 0:LANES] = strip * scale
                out[i, rows, LANES : LANES + 1] = edge[:, back : back + 1]

    queue = [[(unit, role, None) for unit in range(SPLIT)] for role in range(2)]
    for role in range(2):
        for part in range(2):
            queue[role] += [(unit, role, part) for unit in range(SPLIT, len(UNITS))]
    relayout(0, 0)
    relayout(1, 0)
    pl.semaphore_wait(barrier, len(peers) + jnp.where(z < last, 1, 0) + jnp.where(z > 0, 1, 0))
    for item in queue[0][:LEAD]:
        go(to_other(*item))
    relayout(0, 1)
    relayout(1, 1)
    for unit in range(AHEAD):
        go(to_mate(unit))
        keep(unit).start()
    for index in range(len(queue[0]) + LEAD):
        if index >= LEAD:
            go(to_other(*queue[1][index - LEAD]))
        if LEAD <= index < len(queue[0]):
            go(to_other(*queue[0][index]))
        if AHEAD <= index - LEAD + AHEAD < len(UNITS):
            go(to_mate(index - LEAD + AHEAD))
            keep(index - LEAD + AHEAD).start()

    for missing, edge in ((z == 0, 0), (z == last, 2)):

        @pl.when(missing)
        def _(edge=edge):
            def clear(y, carry):
                beside[edge, y] = jnp.zeros((cells, LANES), BF16)
                beside[edge + 1, y] = jnp.zeros((cells, LANES), BF16)
                return carry

            lax.fori_loop(0, QUAD * share, clear, 0, unroll=4)

    forward(0)
    forward(1)
    for unit in range(len(UNITS)):
        if unit + 2 < SPLIT:
            forward(unit + 2)
        if UNITS[unit] == (1, 0):
            finish(0)
        if UNITS[unit] == (4, 0):
            finish(1)
        process(unit)
        if unit + 1 == SPLIT:
            for later in range(SPLIT, len(UNITS)):
                forward(later)
    finish(2)
    land(0)
    finish(3)
    finish(4)
    land(1)

    for copy in sent:
        copy.wait_send()
    for there, upward in ((z < last, True), (z > 0, False)):

        @pl.when(there)
        def _(upward=upward):
            for unit in range(len(UNITS)):
                extend(unit, upward).wait_send()

    @pl.when(jnp.logical_not(sums_here))
    def _():
        for piece in range(len(SIZES)):
            pass_over(UNITS.index((piece, 0))).wait_send()

    @pl.when(sums_here)
    def _():
        for owner in range(QUAD):

            @pl.when(place_in_quad != owner)
            def _(owner=owner):
                for piece in range(len(SIZES)):
                    bring_home(piece, owner).wait_send()
                for group in range(len(GROUPS)):
                    bring_edge(group, owner).wait_send()


def on_device(source, receiver):
    shots, cells, times, cross = source.shape
    all_shots = shots * lax.axis_size("shot")
    block = cross // 8
    share = sum(SIZES)
    wide = QUAD * cells
    scale = 1.0 / (times * all_shots) ** 0.5
    lags = wide + 1
    units, pieces = len(UNITS), len(SIZES)
    image = pl.pallas_call(
        functools.partial(kernel, scale),
        out_shape=pltpu.VMEM((cells, block, lags), F32),
        in_specs=[pl.BlockSpec(memory_space=pl.ANY)] * 2,
        out_specs=pl.BlockSpec(memory_space=pltpu.VMEM),
        scratch_shapes=[
            pltpu.VMEM((2, 2, shots, cells, times, LANES), BF16),
            pltpu.VMEM((cells * LANES, LANES), F32),
            pltpu.VMEM((cross, 2 * cells, LANES), BF16),
            pltpu.VMEM((QUAD, 4 * share, 2 * cells, LANES), BF16),
            pltpu.VMEM((QUAD, 4 * share, cells, LANES), BF16),
            pltpu.VMEM((4 * share * wide + units * SUBLANES, LANES), F32),
            pltpu.VMEM((3, share * wide + pieces * SUBLANES, LANES), F32),
            pltpu.VMEM((share * wide + pieces * SUBLANES, LANES), F32),
            pltpu.VMEM((share, wide, LANES), F32),
            pltpu.VMEM((pieces, SUBLANES, LANES), F32),
            pltpu.VMEM((2, share, cells, LANES), F32),
            pltpu.VMEM((2, pieces, SUBLANES, LANES), F32),
            pltpu.SemaphoreType.DMA((2, 2)),
            pltpu.SemaphoreType.DMA((units,)),
            pltpu.SemaphoreType.DMA((3, 2 * units - SPLIT)),
            pltpu.SemaphoreType.DMA((3, 2 * units - SPLIT)),
            pltpu.SemaphoreType.DMA((2, units)),
            pltpu.SemaphoreType.DMA((2, units)),
            pltpu.SemaphoreType.DMA((3, pieces)),
            pltpu.SemaphoreType.DMA((3, pieces)),
            pltpu.SemaphoreType.DMA((pieces,)),
            pltpu.SemaphoreType.DMA((pieces,)),
            pltpu.SemaphoreType.DMA((QUAD, pieces + len(GROUPS))),
            pltpu.SemaphoreType.DMA((2, pieces + len(GROUPS))),
        ],
        compiler_params=pltpu.CompilerParams(collective_id=0, has_side_effects=True, vmem_limit_bytes=60 * 2**20),
    )(source, receiver)
    return jnp.transpose(image, (2, 0, 1))


def solution(mesh):
    placed = (P("shot", "inline", None, None), P("shot", "inline", None, None))
    return jax.shard_map(
        on_device, mesh=mesh, in_specs=placed, out_specs=P(None, "inline", "shot"), check_vma=False
    )
```

```python
import functools

import jax
import jax.numpy as jnp
from jax import lax
from jax.experimental import pallas as pl
from jax.experimental.pallas import tpu as pltpu
from jax.sharding import PartitionSpec as P

MESH = pl.DeviceIdType.MESH
F32 = jnp.float32
BF16 = jnp.bfloat16
LANES = 128
SUBLANES = 8
RINGS = 4
QUAD = 4
SIZES = (4, 4, 4, 2, 2)
STARTS = (0, 4, 8, 12, 14)
RISING = (True, False, True, False, False)
UNITS = (
    (0, 2), (1, 2), (2, 2), (3, 2), (4, 2), (0, 1), (1, 3), (1, 1), (0, 3), (2, 1),
    (2, 3), (3, 3), (3, 1), (0, 0), (4, 3), (4, 1), (1, 0), (2, 0), (3, 0), (4, 0),
)
GROUPS = ((0, 2), (2, 5))
FIRST = [sum(SIZES[piece] for piece, _ in UNITS[:unit]) for unit in range(len(UNITS))]
FAR, SUM, NEAR = range(3)
AHEAD = 2
LEAD = 3
SPLIT = len(UNITS) - 9


def kernel(
    scale, source, receiver, out,
    raw, turned, own, held, beside, partial, inbox, across, total, total_edge, landed, landed_edge,
    raw_sem, own_sem, ship_send, ship_recv, along_send, along_recv, ring_send, ring_recv,
    over_send, over_recv, home_send, home_recv,
):
    shots, cells, times, _ = source.shape
    share = sum(SIZES)
    wide = QUAD * cells
    owners = lax.axis_size("inline")
    me, shot = lax.axis_index("inline"), lax.axis_index("shot")
    core, low, x, high = me % 2, (me // 2) % 2, shot % RINGS, shot // RINGS
    place_in_quad, z = me % QUAD, me // QUAD
    quad = z * QUAD
    core_mate = me + 1 - 2 * core
    low_mate = me + 2 - 4 * low
    above = (me + QUAD) % owners
    below = (me + owners - QUAD) % owners
    up = high * RINGS + (x + 1) % RINGS
    down = high * RINGS + (x + RINGS - 1) % RINGS
    high_mate = (1 - high) * RINGS + x
    diagonal = low_mate + 1 - 2 * core
    peers = [
        (core_mate, shot), (low_mate, shot), (diagonal, shot), (me, up), (me, down), (low_mate, high_mate),
    ]
    last = owners // QUAD - 1
    sums_here = low == core

    def place(inline, line):
        return {"inline": inline, "shot": line}

    loads = []
    tiles = [pl.multiple_of(((high + 1 + role) % 2) * LANES, LANES) for role in range(2)]
    for tile in range(2):
        for which, array in enumerate((receiver, source)):
            loads.append(
                pltpu.make_async_copy(
                    array.at[:, :, :, pl.ds(tiles[tile], LANES)], raw.at[which, tile], raw_sem.at[which, tile]
                )
            )
            loads[-1].start()

    barrier = pltpu.get_barrier_semaphore()
    for inline, line in peers:
        pl.semaphore_signal(barrier, inc=1, device_id=place(inline, line), device_id_type=MESH)
    for there, inline in ((z < last, above), (z > 0, below)):

        @pl.when(there)
        def _(inline=inline):
            pl.semaphore_signal(barrier, inc=1, device_id=place(inline, shot), device_id_type=MESH)

    def relayout(which, tile):
        loads[2 * tile + which].wait()

        def turn(i, carry):
            rows = jnp.concatenate([raw[which, tile, s, i] for s in range(shots)], axis=0)
            row = cells - 1 - i if which else i
            turned[pl.ds(pl.multiple_of(row * LANES, LANES), LANES), :] = rows.T.astype(F32)
            return carry

        def gather(y, carry):
            own[tiles[tile] + y, which * cells : (which + 1) * cells] = turned[pl.ds(y, cells, stride=LANES), :].astype(BF16)
            return carry

        lax.fori_loop(0, cells, turn, 0, unroll=8)
        lax.fori_loop(0, LANES, gather, 0, unroll=16)

    def rows_from(unit, half, target_core):
        piece, hop = UNITS[unit]
        start = half * LANES + ((x + hop) % RINGS) * 2 * share + target_core * share + STARTS[piece]
        return pl.ds(start, SIZES[piece])

    def rows_to(unit):
        return pl.ds(FIRST[unit], SIZES[UNITS[unit][0]])

    def ship(unit, half, target, target_core, sent_as, received_as, part=None):
        inner = pl.ds(0, 2 * cells) if part is None else pl.ds(part * cells, cells)
        column = len(UNITS) + unit - SPLIT if part else unit
        return pltpu.make_async_remote_copy(
            src_ref=own.at[rows_from(unit, half, target_core), inner],
            dst_ref=held.at[place_in_quad, rows_to(unit), inner],
            send_sem=ship_send.at[sent_as, column],
            recv_sem=ship_recv.at[received_as, column],
            device_id=place(target, shot),
            device_id_type=MESH,
        )

    def to_mate(unit):
        return ship(unit, (low + high + 1 - core) % 2, core_mate, 1 - core, 0, 0)

    def to_other(unit, role, part=None):
        target_core = (role - low) % 2
        target = quad + 2 * (1 - low) + target_core
        return ship(unit, (high + 1 + role) % 2, target, target_core, 1 + role, 1 + core, part)

    def from_other(unit, part=None):
        for sender in range(2):
            ship(unit, 0, low_mate, core, 1, 1 + sender, part).wait_recv()

    def keep(unit):
        return pltpu.make_async_copy(
            own.at[rows_from(unit, (low + high + core) % 2, core)],
            held.at[place_in_quad, rows_to(unit)],
            own_sem.at[unit],
        )

    def extend(unit, upward):
        rows = rows_to(unit)
        begin, end = (2, 0) if upward else (0, 2)
        return pltpu.make_async_remote_copy(
            src_ref=held.at[pl.ds(begin, 2), rows, pl.ds(0, cells)],
            dst_ref=beside.at[pl.ds(end, 2), rows],
            send_sem=along_send.at[int(upward), unit],
            recv_sem=along_recv.at[int(upward), unit],
            device_id=place(above if upward else below, shot),
            device_id_type=MESH,
        )

    def unit_rows(unit):
        return pl.ds(FIRST[unit] * wide + unit * SUBLANES, SIZES[UNITS[unit][0]] * wide + SUBLANES)

    def piece_rows(piece):
        return pl.ds(STARTS[piece] * wide + piece * SUBLANES, SIZES[piece] * wide + SUBLANES)

    def ring(kind, unit, line):
        piece, _ = UNITS[unit]
        return pltpu.make_async_remote_copy(
            src_ref=partial.at[unit_rows(unit)],
            dst_ref=inbox.at[kind, piece_rows(piece)],
            send_sem=ring_send.at[kind, piece],
            recv_sem=ring_recv.at[kind, piece],
            device_id=place(me, line),
            device_id_type=MESH,
        )

    lane = lax.broadcasted_iota(jnp.int32, (wide, LANES), 1)
    straight = lane <= lax.broadcasted_iota(jnp.int32, (wide, LANES), 0)

    def correlate(unit, kinds):
        piece, _ = UNITS[unit]
        size = SIZES[piece]
        begin, begin_in = FIRST[unit] * wide + unit * SUBLANES, STARTS[piece] * wide + piece * SUBLANES

        edge = jnp.zeros((wide, LANES), F32)
        for m in range(size):
            y = FIRST[unit] + m
            contract = (((1,), (1,)), ((), ()))
            rows = jnp.concatenate([held[QUAD - 1 - part, y, cells:] for part in range(QUAD)], axis=0)
            columns = [beside[0, y], beside[1, y]] + [held[part, y, :cells] for part in range(QUAD)]
            columns = jnp.concatenate(columns + [beside[2, y], beside[3, y]], axis=0)
            product = lax.dot_general(rows, columns, contract, preferred_element_type=F32)
            a = pltpu.roll(product[:, 0:LANES], 1, axis=1, stride=1, stride_axis=0)
            b = pltpu.roll(product[:, LANES:], 1, axis=1, stride=1, stride_axis=0)
            band = jnp.where(straight, a, b)
            for kind in kinds:
                band = band + inbox[kind, begin_in + m * wide : begin_in + (m + 1) * wide, :]
            partial[begin + m * wide : begin + (m + 1) * wide, :] = band
            spot = STARTS[piece] % SUBLANES + m
            edge = jnp.where(lane == spot, pltpu.roll(b, spot, axis=1) if spot else b, edge)
        edge = edge.T[0:SUBLANES]
        for kind in kinds:
            edge = edge + inbox[kind, begin_in + size * wide : begin_in + size * wide + SUBLANES, :]
        partial[begin + size * wide : begin + size * wide + SUBLANES, :] = edge

    sent = []

    def go(copy):
        copy.start()
        sent.append(copy)

    def pass_over(unit):
        piece, _ = UNITS[unit]
        return pltpu.make_async_remote_copy(
            src_ref=partial.at[unit_rows(unit)],
            dst_ref=across.at[piece_rows(piece)],
            send_sem=over_send.at[piece],
            recv_sem=over_recv.at[piece],
            device_id=place(low_mate, high_mate),
            device_id_type=MESH,
        )

    def process(unit):
        if unit >= SPLIT:
            from_other(unit, 1)

        @pl.when(z > 0)
        def _():
            extend(unit, True).wait_recv()

        @pl.when(z < last)
        def _():
            extend(unit, False).wait_recv()

        piece, hop = UNITS[unit]
        rising = RISING[piece]
        toward = up if rising else down
        if hop == 2:
            correlate(unit, ())
            go(ring(FAR, unit, toward))
        elif hop == 0:
            ring(SUM, unit, toward).wait_recv()
            ring(NEAR, unit, toward).wait_recv()
            correlate(unit, (SUM, NEAR))

            @pl.when(jnp.logical_not(sums_here))
            def _():
                pass_over(unit).start()
        elif (hop == 1) == rising:
            ring(FAR, unit, toward).wait_recv()
            correlate(unit, (FAR,))
            go(ring(SUM, unit, toward))
        else:
            correlate(unit, ())
            go(ring(NEAR, unit, down if rising else up))

    def bring_home(piece, owner):
        rows = pl.ds(STARTS[piece], SIZES[piece])
        return pltpu.make_async_remote_copy(
            src_ref=total.at[rows, pl.ds((QUAD - 1 - owner) * cells, cells)],
            dst_ref=landed.at[core, rows],
            send_sem=home_send.at[owner, piece],
            recv_sem=home_recv.at[core, piece],
            device_id=place(quad + owner, shot),
            device_id_type=MESH,
        )

    def bring_edge(group, owner):
        rows = pl.ds(GROUPS[group][0], GROUPS[group][1] - GROUPS[group][0])
        return pltpu.make_async_remote_copy(
            src_ref=total_edge.at[rows],
            dst_ref=landed_edge.at[core, rows],
            send_sem=home_send.at[owner, len(SIZES) + group],
            recv_sem=home_recv.at[core, len(SIZES) + group],
            device_id=place(quad + owner, shot),
            device_id_type=MESH,
        )

    def finish(piece):
        unit = UNITS.index((piece, 0))
        size = SIZES[piece]
        begin, begin_in = FIRST[unit] * wide + unit * SUBLANES, STARTS[piece] * wide + piece * SUBLANES

        @pl.when(sums_here)
        def _():
            pass_over(unit).wait_recv()
            for m in range(size):
                total[STARTS[piece] + m] = (
                    partial[begin + m * wide : begin + (m + 1) * wide, :]
                    + across[begin_in + m * wide : begin_in + (m + 1) * wide, :]
                )
            edge = (
                partial[begin + size * wide : begin + size * wide + SUBLANES, :]
                + across[begin_in + size * wide : begin_in + size * wide + SUBLANES, :]
            )
            total_edge[piece] = edge
            for owner in (2, 3, 0, 1):

                @pl.when(place_in_quad != owner)
                def _(owner=owner):
                    bring_home(piece, owner).start()
                    for group, (_, stop) in enumerate(GROUPS):
                        if piece == stop - 1:
                            bring_edge(group, owner).start()

                @pl.when(place_in_quad == owner)
                def _(owner=owner):
                    rows = slice(STARTS[piece], STARTS[piece] + size)
                    cut = slice((QUAD - 1 - owner) * cells, (QUAD - owner) * cells)
                    landed[core, rows] = total[rows, cut]
                    landed_edge[core, piece] = edge

    def forward(unit):
        keep(unit).wait()
        to_mate(unit).wait_recv()
        from_other(unit, 0 if unit >= SPLIT else None)

        @pl.when(z < last)
        def _():
            extend(unit, True).start()

        @pl.when(z > 0)
        def _():
            extend(unit, False).start()


    def land(group):
        pieces = range(*GROUPS[group])
        for summer in range(2):

            @pl.when(place_in_quad != (QUAD - 1) * summer)
            def _(summer=summer):
                for piece in pieces:
                    rows = pl.ds(STARTS[piece], SIZES[piece])
                    pltpu.make_async_remote_copy(
                        src_ref=total.at[rows, pl.ds(0, cells)],
                        dst_ref=landed.at[summer, rows],
                        send_sem=home_send.at[0, piece],
                        recv_sem=home_recv.at[summer, piece],
                        device_id=place(low_mate, shot),
                        device_id_type=MESH,
                    ).wait_recv()
                rows = pl.ds(GROUPS[group][0], GROUPS[group][1] - GROUPS[group][0])
                pltpu.make_async_remote_copy(
                    src_ref=total_edge.at[rows],
                    dst_ref=landed_edge.at[summer, rows],
                    send_sem=home_send.at[0, len(SIZES) + group],
                    recv_sem=home_recv.at[summer, len(SIZES) + group],
                    device_id=place(low_mate, shot),
                    device_id_type=MESH,
                ).wait_recv()

            edge = sum(landed_edge[summer, piece] for piece in pieces) * scale
            edge = pltpu.roll(edge, (place_in_quad + 1) * cells, axis=1)
            rows = pl.ds(summer * share + group * SUBLANES, SUBLANES)
            for i in range(cells):
                back = cells - 1 - i
                strip = landed[summer, group * SUBLANES : (group + 1) * SUBLANES, back, :]
                out[i, rows, 0:LANES] = strip * scale
                out[i, rows, LANES : LANES + 1] = edge[:, back : back + 1]

    queue = [[(unit, role, None) for unit in range(SPLIT)] for role in range(2)]
    for role in range(2):
        for part in range(2):
            queue[role] += [(unit, role, part) for unit in range(SPLIT, len(UNITS))]
    relayout(0, 0)
    relayout(1, 0)
    pl.semaphore_wait(barrier, len(peers) + jnp.where(z < last, 1, 0) + jnp.where(z > 0, 1, 0))
    for item in queue[0][:LEAD]:
        go(to_other(*item))
    relayout(0, 1)
    relayout(1, 1)
    for unit in range(AHEAD):
        go(to_mate(unit))
        keep(unit).start()
    for index in range(len(queue[0]) + LEAD):
        if index >= LEAD:
            go(to_other(*queue[1][index - LEAD]))
        if LEAD <= index < len(queue[0]):
            go(to_other(*queue[0][index]))
        if AHEAD <= index - LEAD + AHEAD < len(UNITS):
            go(to_mate(index - LEAD + AHEAD))
            keep(index - LEAD + AHEAD).start()

    for missing, edge in ((z == 0, 0), (z == last, 2)):

        @pl.when(missing)
        def _(edge=edge):
            def clear(y, carry):
                beside[edge, y] = jnp.zeros((cells, LANES), BF16)
                beside[edge + 1, y] = jnp.zeros((cells, LANES), BF16)
                return carry

            lax.fori_loop(0, QUAD * share, clear, 0, unroll=4)

    forward(0)
    forward(1)
    for unit in range(len(UNITS)):
        if unit + 2 < SPLIT:
            forward(unit + 2)
        if UNITS[unit] == (1, 0):
            finish(0)
        if UNITS[unit] == (4, 0):
            finish(1)
        process(unit)
        if unit + 1 == SPLIT:
            for later in range(SPLIT, len(UNITS)):
                forward(later)
    finish(2)
    land(0)
    finish(3)
    finish(4)
    land(1)

    for copy in sent:
        copy.wait_send()
    for there, upward in ((z < last, True), (z > 0, False)):

        @pl.when(there)
        def _(upward=upward):
            for unit in range(len(UNITS)):
                extend(unit, upward).wait_send()

    @pl.when(jnp.logical_not(sums_here))
    def _():
        for piece in range(len(SIZES)):
            pass_over(UNITS.index((piece, 0))).wait_send()

    @pl.when(sums_here)
    def _():
        for owner in range(QUAD):

            @pl.when(place_in_quad != owner)
            def _(owner=owner):
                for piece in range(len(SIZES)):
                    bring_home(piece, owner).wait_send()
                for group in range(len(GROUPS)):
                    bring_edge(group, owner).wait_send()


def on_device(source, receiver):
    shots, cells, times, cross = source.shape
    all_shots = shots * lax.axis_size("shot")
    block = cross // 8
    share = sum(SIZES)
    wide = QUAD * cells
    scale = 1.0 / (times * all_shots) ** 0.5
    lags = wide + 1
    units, pieces = len(UNITS), len(SIZES)
    image = pl.pallas_call(
        functools.partial(kernel, scale),
        out_shape=pltpu.VMEM((cells, block, lags), F32),
        in_specs=[pl.BlockSpec(memory_space=pl.ANY)] * 2,
        out_specs=pl.BlockSpec(memory_space=pltpu.VMEM),
        scratch_shapes=[
            pltpu.VMEM((2, 2, shots, cells, times, LANES), BF16),
            pltpu.VMEM((cells * LANES, LANES), F32),
            pltpu.VMEM((cross, 2 * cells, LANES), BF16),
            pltpu.VMEM((QUAD, 4 * share, 2 * cells, LANES), BF16),
            pltpu.VMEM((QUAD, 4 * share, cells, LANES), BF16),
            pltpu.VMEM((4 * share * wide + units * SUBLANES, LANES), F32),
            pltpu.VMEM((3, share * wide + pieces * SUBLANES, LANES), F32),
            pltpu.VMEM((share * wide + pieces * SUBLANES, LANES), F32),
            pltpu.VMEM((share, wide, LANES), F32),
            pltpu.VMEM((pieces, SUBLANES, LANES), F32),
            pltpu.VMEM((2, share, cells, LANES), F32),
            pltpu.VMEM((2, pieces, SUBLANES, LANES), F32),
            pltpu.SemaphoreType.DMA((2, 2)),
            pltpu.SemaphoreType.DMA((units,)),
            pltpu.SemaphoreType.DMA((3, 2 * units - SPLIT)),
            pltpu.SemaphoreType.DMA((3, 2 * units - SPLIT)),
            pltpu.SemaphoreType.DMA((2, units)),
            pltpu.SemaphoreType.DMA((2, units)),
            pltpu.SemaphoreType.DMA((3, pieces)),
            pltpu.SemaphoreType.DMA((3, pieces)),
            pltpu.SemaphoreType.DMA((pieces,)),
            pltpu.SemaphoreType.DMA((pieces,)),
            pltpu.SemaphoreType.DMA((QUAD, pieces + len(GROUPS))),
            pltpu.SemaphoreType.DMA((2, pieces + len(GROUPS))),
        ],
        compiler_params=pltpu.CompilerParams(collective_id=0, has_side_effects=True, vmem_limit_bytes=60 * 2**20),
    )(source, receiver)
    return jnp.transpose(image, (2, 0, 1))


def solution(mesh):
    placed = (P("shot", "inline", None, None), P("shot", "inline", None, None))
    return jax.shard_map(
        on_device, mesh=mesh, in_specs=placed, out_specs=P(None, "inline", "shot"), check_vma=False
    )
```
